512 devices in a mesh: seq: 128 (over z, y, x_hi), branch: 4 (over x_lo, core).
Axes of the slice: x: 4 (x_hi: 2, x_lo: 2; x = x_hi * 2 + x_lo), y: 4, z: 16, core: 2. Of those that a mesh axis runs over, the one named last changes fastest.
Arguments:
- q_ctl: bfloat16 [4, 24576, 2048], P('branch', 'seq'), may hold values from -64 to 64
- k_ctl: bfloat16 [4, 24576, 2048], P('branch', 'seq'), may hold values from -64 to 64
- v_ctl: bfloat16 [4, 24576, 2048], P('branch', 'seq'), may hold values from -6 to 6
- positions: int32 [24576], P('seq'), may hold values from 0 to 12287
- branch_ids: int32 [4], P('branch'), may hold values from 0 to 63
- cond_scale: float32 [64], replicated, may hold values from 0.25 to 2
- out_weight: bfloat16 [2048, 3072], P('branch', 'seq'), may hold values from -0.125 to 0.125
- frozen: bfloat16 [24576, 3072], P(('seq', 'branch')), may hold values from -2.390625 to 2.390625
- norm_gain: float32 [3072], replicated, may hold values from 0.5 to 1.5
- cotangent: bfloat16 [24576, 3072], P('seq'), may hold values from -6 to 6
Outputs:
- normed: bfloat16 [24576, 3072], P(('seq', 'branch'))
- grad_attn: bfloat16 [4, 24576, 2048], P('branch', 'seq')
The draws below stay inside these ranges and needn't reach their ends.
All inputs are finite; a program needn't handle non-finite values.
Results may differ from the reference program's by a relative error of at most 0.014.
Values may be sent and summed in bfloat16 or wider, within the bound.
No kernel may reach another device: no remote copies, remote signals or barrier semaphores. Data moves between devices by JAX's collectives and lax.ppermute only.
A program may use at most 64 MiB of HBM per device.

```python
import math
import jax
import jax.numpy as jnp
from jax import lax

D = 3072
HEADS = 16
HEAD_DIM = 128
CONDS = 4
ADAPTERS = 64
HD = 2048
LEN = 3072
SEQS = 8
TOKENS = 24576


def query_key_pair(key):
    full_shape = (CONDS, TOKENS, HD)
    key_part = jnp.clip(jax.random.normal(jax.random.fold_in(key, 21), full_shape, jnp.float32), -6.0, 6.0)
    query_part = 2.0 * jnp.clip(jax.random.normal(jax.random.fold_in(key, 22), full_shape, jnp.float32), -6.0, 6.0)
    return (query_part, key_part)


def draw_q_ctl(key, part):
    return query_key_pair(key)[0].astype(jnp.bfloat16)


def draw_k_ctl(key, part):
    return query_key_pair(key)[1].astype(jnp.bfloat16)


def set_ends(values, own_key, least, top_value):
    longest = values.shape.index(max(values.shape))
    spots = []
    for shift in (0, 1):
        where = [jax.random.randint(jax.random.fold_in(own_key, axis), (), 0, length) for axis, length in enumerate(values.shape)]
        where[longest] = (where[longest] + shift) % values.shape[longest]
        spots.append(tuple(where))
    return values.at[spots[0]].set(least).at[spots[1]].set(top_value)


def steps_of(own_key, extent, split, low, top_value):
    gain, own = 1.0, jax.random.fold_in(own_key, 6)
    for position, parts in split:
        heights = jnp.exp(jax.random.uniform(jax.random.fold_in(own, position), (parts,), jnp.float32, low / len(split), top_value / len(split)))
        gain = gain * jnp.repeat(heights, extent[position] // parts).reshape([-1 if axis == position else 1 for axis in range(len(extent))])
    return gain


def noise(stream_key, dims, deviation, limit, pieces=(), kind=jnp.bfloat16):
    factor_of = steps_of(stream_key, dims, pieces, -0.22, 0.18) if pieces else 1.0
    entries = jax.random.normal(stream_key, dims, jnp.float32) * deviation * factor_of
    return jnp.minimum(jnp.maximum(entries, -limit), limit).astype(kind)


def setup_inputs(seed: int = 0) -> dict:
    arg_keys = jax.random.split(jax.random.key(seed), 11)
    q_ctl = draw_q_ctl(jax.random.fold_in(arg_keys[10], 71), 0)
    k_ctl = draw_k_ctl(jax.random.fold_in(arg_keys[10], 71), 0)
    v_ctl = noise(arg_keys[2], (CONDS, TOKENS, HD), 1.0, 6.0, ((0, 4), (1, 128)))
    positions = set_ends(jax.random.randint(arg_keys[3], (TOKENS,), 0, 4 * LEN), jax.random.fold_in(arg_keys[3], 1), 0, (4 * LEN) - 1).astype(jnp.int32)
    branch_ids = set_ends(jax.random.randint(arg_keys[4], (CONDS,), 0, ADAPTERS), jax.random.fold_in(arg_keys[4], 1), 0, ADAPTERS - 1).astype(jnp.int32)
    cond_scale = jnp.clip(jnp.exp(jax.random.uniform(arg_keys[5], (ADAPTERS,), jnp.float32, math.log(0.25), math.log(2.0))), 0.25, 2.0)
    out_weight = noise(arg_keys[6], (HD, D), HD ** -0.5, 0.125, ((0, 4), (1, 128)))
    frozen = noise(arg_keys[7], (TOKENS, D), 0.3, 2.390625, ((0, 512),))
    norm_gain = jnp.clip(1.0 + 0.1 * jax.random.normal(arg_keys[8], (D,), jnp.float32), 0.5, 1.5)
    cotangent = noise(arg_keys[9], (TOKENS, D), 1.0, 6.0, ((0, 128),))
    return dict(q_ctl=q_ctl, k_ctl=k_ctl, v_ctl=v_ctl, positions=positions, branch_ids=branch_ids, cond_scale=cond_scale, out_weight=out_weight, frozen=frozen, norm_gain=norm_gain, cotangent=cotangent)


EPS = 1e-06

def rope_tables(positions, head_dim):
    exponents = jnp.arange(head_dim // 2, dtype=jnp.float32) * (2.0 / head_dim)
    frequencies = 10000.0 ** (-exponents)
    angles = positions.astype(jnp.float32)[..., None] * frequencies
    return (jnp.cos(angles), jnp.sin(angles))

def rotate(values_in, cosines, sines):
    half_dim = values_in.shape[-1] // 2
    front_half = values_in[..., :half_dim]
    back_half = values_in[..., half_dim:]
    return jnp.concatenate([front_half * cosines - back_half * sines, back_half * cosines + front_half * sines], axis=-1)

def normalize(hidden, norm_gain):
    inverse = lax.rsqrt(lax.optimization_barrier(jnp.mean(hidden * hidden, axis=-1, keepdims=True)) + EPS)
    return (hidden * inverse * norm_gain).astype(jnp.bfloat16)

def norm_grad(hidden, norm_gain, cotangent):
    inverse = lax.rsqrt(lax.optimization_barrier(jnp.mean(hidden * hidden, axis=-1, keepdims=True)) + EPS)
    upstream = cotangent.astype(jnp.float32) * norm_gain
    inner_mean = lax.optimization_barrier(jnp.mean(upstream * hidden, axis=-1, keepdims=True))
    return (inverse * upstream - hidden * (inverse * inverse * inverse) * inner_mean).astype(jnp.bfloat16)

def attend_one(one_item):
    query_rows, key_rows, value_rows = one_item
    scores = jnp.dot(query_rows, key_rows.T, preferred_element_type=jnp.float32) * (1.0 / math.sqrt(query_rows.shape[-1]))
    row_max = lax.optimization_barrier(jnp.max(scores, axis=-1, keepdims=True))
    weights = jnp.exp(scores - row_max)
    row_total = lax.optimization_barrier(jnp.sum(weights, axis=-1, keepdims=True))
    weights_low = (weights / row_total).astype(jnp.bfloat16)
    return jnp.dot(weights_low, value_rows, preferred_element_type=jnp.float32).astype(jnp.bfloat16)

def reference(q_ctl, k_ctl, v_ctl, positions, branch_ids, cond_scale, out_weight, frozen, norm_gain, cotangent):
    cosines, sines = rope_tables(positions, HEAD_DIM)
    cosines = cosines[None, :, None, :]
    sines = sines[None, :, None, :]

    def rotated(source):
        split_heads = source.astype(jnp.float32).reshape(CONDS, TOKENS, HEADS, HEAD_DIM)
        return rotate(split_heads, cosines, sines).astype(jnp.bfloat16)

    def as_items(split_heads):
        grouped = split_heads.reshape(CONDS, SEQS, LEN, HEADS, HEAD_DIM)
        return jnp.transpose(grouped, (0, 1, 3, 2, 4)).reshape(CONDS * SEQS * HEADS, LEN, HEAD_DIM)
    query_items = as_items(rotated(q_ctl))
    key_items = as_items(rotated(k_ctl))
    value_items = as_items(v_ctl.reshape(CONDS, TOKENS, HEADS, HEAD_DIM))
    outputs = lax.map(attend_one, (query_items, key_items, value_items))
    attended = jnp.transpose(outputs.reshape(CONDS, SEQS, HEADS, LEN, HEAD_DIM), (0, 1, 3, 2, 4)).reshape(CONDS, TOKENS, HD)
    branch_scale = cond_scale[branch_ids]

    def accumulate(carry, pair):
        scale_one, attended_one = pair
        return (carry + scale_one * jnp.dot(attended_one, out_weight, preferred_element_type=jnp.float32), None)
    start_stream = frozen.astype(jnp.float32)
    hidden, unused = lax.scan(accumulate, start_stream, (branch_scale, attended))
    normed = normalize(hidden, norm_gain)
    grad_hidden = norm_grad(hidden, norm_gain, cotangent)
    cot_attn = jnp.dot(grad_hidden, out_weight.T, preferred_element_type=jnp.float32).astype(jnp.bfloat16)
    grad_attn = (branch_scale[:, None, None] * cot_attn.astype(jnp.float32)[None]).astype(jnp.bfloat16)
    return (normed, grad_attn)
```

```python
import math

import jax
import jax.numpy as jnp
from jax import lax
from jax.experimental import pallas as pl
from jax.experimental.pallas import tpu as pltpu
from jax.sharding import Mesh
from jax.sharding import PartitionSpec as P

HEADS = 16
HEAD_DIM = 128
EPS = 1e-06
CLIP = ("z", "y", "h")
SEQ = ("c", "z", "y", "h")
BRANCH = ("l", "k")
F32 = jnp.float32
BF16 = jnp.bfloat16
NT = (((1,), (1,)), ((), ()))


def rope_tables(positions):
    exponents = jnp.arange(HEAD_DIM // 2, dtype=F32) * (2.0 / HEAD_DIM)
    angles = positions.astype(F32)[:, None] * (10000.0 ** (-exponents))
    cosines, sines = jnp.cos(angles), jnp.sin(angles)
    return (
        jnp.concatenate([cosines, cosines], axis=1),
        jnp.concatenate([-sines, sines], axis=1),
    )


def prepare(q, k, v, cosines, sines):
    rows = q.shape[0]
    factor = math.log2(math.e) / math.sqrt(HEAD_DIM)

    def kernel(q_ref, k_ref, v_ref, c_ref, s_ref, o_ref):
        c, s = c_ref[...], s_ref[...]

        def rotated(x):
            x = x.astype(F32)
            return x * c + pltpu.roll(x, HEAD_DIM // 2, 1) * s

        o_ref[0, 0:rows, :] = (rotated(q_ref[...]) * factor).astype(BF16)
        o_ref[0, rows : 2 * rows, :] = rotated(k_ref[...]).astype(BF16)
        o_ref[0, 2 * rows :, :] = v_ref[...]

    column = pl.BlockSpec((rows, HEAD_DIM), lambda i: (0, i))
    whole = pl.BlockSpec((rows, HEAD_DIM), lambda i: (0, 0))
    return pl.pallas_call(
        kernel,
        out_shape=jax.ShapeDtypeStruct((HEADS, 3 * rows, HEAD_DIM), BF16),
        grid=(HEADS,),
        in_specs=[column, column, column, whole, whole],
        out_specs=pl.BlockSpec((1, 3 * rows, HEAD_DIM), lambda i: (i, 0, 0)),
        name="prepare",
    )(q, k, v, cosines, sines)


def attend(blocks, scale):
    sources, three_rows, _ = blocks.shape
    rows = three_rows // 3
    length = sources * rows
    bq, kc, kt = 512, 512, 256
    steps = length // bq

    def kernel(scale_ref, b_ref, o_ref, q_ref, k_ref, v_ref, s_ref, m_ref):
        for j in range(sources):
            at = slice(j * rows, (j + 1) * rows)
            q_ref[at, :] = b_ref[j, 0:rows, :]
            k_ref[at, :] = b_ref[j, rows : 2 * rows, :]
            v_ref[at, 0:HEAD_DIM] = b_ref[j, 2 * rows :, :]
        v_ref[:, HEAD_DIM:] = jnp.ones((length, HEAD_DIM), BF16)

        def scores(i, slot):
            q = q_ref[pl.ds(pl.multiple_of(i * bq, bq), bq), :]
            top = None
            for j in range(length // kt):
                s = lax.dot_general(
                    q, k_ref[j * kt : (j + 1) * kt, :], NT, preferred_element_type=F32
                )
                s_ref[slot, :, j * kt : (j + 1) * kt] = s
                for half in range(kt // 128):
                    part = s[:, half * 128 : (half + 1) * 128]
                    top = part if top is None else jnp.maximum(top, part)
            m_ref[slot] = jnp.broadcast_to(jnp.max(top, axis=1, keepdims=True), (bq, 128))

        def mix(i, slot):
            top = jnp.concatenate([m_ref[slot]] * (kc // 128), axis=1)
            total = None
            for j in range(length // kc):
                p = jnp.exp2(s_ref[slot, :, j * kc : (j + 1) * kc] - top).astype(BF16)
                part = jnp.dot(p, v_ref[j * kc : (j + 1) * kc, :], preferred_element_type=F32)
                total = part if total is None else total + part
            out = total[:, :HEAD_DIM] * (scale_ref[0] / total[:, HEAD_DIM:])
            o_ref[pl.ds(pl.multiple_of(i * bq, bq), bq), :] = out.astype(BF16)

        scores(0, 0)

        def pair(t, carry):
            i = 2 * t
            scores(i + 1, 1)
            mix(i, 0)
            scores(i + 2, 0)
            mix(i + 1, 1)
            return carry

        lax.fori_loop(0, (steps - 2) // 2, pair, 0)
        scores(steps - 1, 1)
        mix(steps - 2, 0)
        mix(steps - 1, 1)

    return pl.pallas_call(
        kernel,
        out_shape=jax.ShapeDtypeStruct((length, HEAD_DIM), BF16),
        in_specs=[
            pl.BlockSpec(memory_space=pltpu.SMEM),
            pl.BlockSpec(memory_space=pltpu.VMEM),
        ],
        out_specs=pl.BlockSpec(memory_space=pltpu.VMEM),
        scratch_shapes=[
            pltpu.VMEM((length, HEAD_DIM), BF16),
            pltpu.VMEM((length, HEAD_DIM), BF16),
            pltpu.VMEM((length, 2 * HEAD_DIM), BF16),
            pltpu.VMEM((2, bq, length), F32),
            pltpu.VMEM((2, bq, 128), F32),
        ],
        compiler_params=pltpu.CompilerParams(vmem_limit_bytes=48 << 20),
        name="attend",
    )(scale, blocks)


def on_device(
    q_ctl, k_ctl, v_ctl, positions, branch_ids, cond_scale, out_weight, frozen, norm_gain, cotangent
):
    branch = lax.axis_index(BRANCH)
    share = frozen.shape[0]
    width = frozen.shape[1]
    scale = jnp.sum(jnp.where(jnp.arange(cond_scale.shape[0]) == branch_ids[0], cond_scale, 0.0))

    weight_t = lax.all_gather(out_weight.T, SEQ + BRANCH, axis=0, tiled=True)
    weight_t = weight_t.reshape(width // out_weight.shape[1], 4, out_weight.shape[1], -1)
    weight_t = jnp.transpose(weight_t, (0, 2, 1, 3)).reshape(width, -1)

    cosines, sines = rope_tables(positions)
    blocks = prepare(q_ctl[0], k_ctl[0], v_ctl[0], cosines, sines)
    blocks = lax.all_to_all(blocks, CLIP, 0, 0, tiled=True)
    attended = attend(blocks, scale.reshape(1))
    pieces = lax.all_to_all(
        attended.reshape(HEADS * 4, share, HEAD_DIM), CLIP + BRANCH, 0, 0, tiled=True
    )
    mixed = jnp.sum(pieces.reshape(HEADS, 4, share, HEAD_DIM).astype(F32), axis=1)
    mixed = jnp.transpose(mixed, (1, 0, 2)).reshape(share, -1).astype(BF16)

    hidden = frozen.astype(F32) + lax.dot_general(mixed, weight_t, NT, preferred_element_type=F32)
    inverse = lax.rsqrt(jnp.mean(hidden * hidden, axis=-1, keepdims=True) + EPS)
    normed = (hidden * inverse * norm_gain).astype(BF16)
    upstream = lax.dynamic_slice_in_dim(cotangent, branch * share, share, 0).astype(F32) * norm_gain
    inner = jnp.mean(upstream * hidden, axis=-1, keepdims=True)
    grad = (inverse * upstream - hidden * (inverse * inverse * inverse) * inner).astype(BF16)
    cot = jnp.dot(grad, weight_t, preferred_element_type=F32).astype(BF16)
    cot = lax.all_gather(cot, BRANCH, axis=0, tiled=True)
    grad_attn = (scale * cot.astype(F32)).astype(BF16)
    return normed, grad_attn[None]


def solution(mesh):
    fine = Mesh(mesh.devices.reshape(8, 2, 4, 2, 2, 2), SEQ + BRANCH)
    return jax.shard_map(
        on_device,
        mesh=fine,
        in_specs=(
            P(BRANCH, SEQ, None),
            P(BRANCH, SEQ, None),
            P(BRANCH, SEQ, None),
            P(SEQ),
            P(BRANCH),
            P(),
            P(BRANCH, SEQ),
            P(SEQ + BRANCH, None),
            P(),
            P(SEQ, None),
        ),
        out_specs=(P(SEQ + BRANCH, None), P(BRANCH, SEQ, None)),
        check_vma=False,
    )
```

```python
import math

import jax
import jax.numpy as jnp
from jax import lax
from jax.experimental import pallas as pl
from jax.experimental.pallas import tpu as pltpu
from jax.sharding import Mesh
from jax.sharding import PartitionSpec as P


HEADS = 16
HEAD_DIM = 128
EPS = 1e-06
CLIP = ("z", "y", "h")
SEQ = ("c", "z", "y", "h")
BRANCH = ("l", "k")
F32 = jnp.float32
BF16 = jnp.bfloat16
NT = (((1,), (1,)), ((), ()))


def rope_tables(positions):
    exponents = jnp.arange(HEAD_DIM // 2, dtype=F32) * (2.0 / HEAD_DIM)
    angles = positions.astype(F32)[:, None] * (10000.0 ** (-exponents))
    cosines, sines = jnp.cos(angles), jnp.sin(angles)
    return (
        jnp.concatenate([cosines, cosines], axis=1),
        jnp.concatenate([-sines, sines], axis=1),
    )


def prepare(q, k, v, cosines, sines):
    rows = q.shape[0]
    factor = math.log2(math.e) / math.sqrt(HEAD_DIM)
    group = 4

    def kernel(q_ref, k_ref, v_ref, c_ref, s_ref, o_ref):
        c, s = c_ref[...], s_ref[...]
        cq, sq = c * factor, s * factor
        for g in range(group):
            at = slice(g * HEAD_DIM, (g + 1) * HEAD_DIM)
            x = q_ref[:, at].astype(F32)
            o_ref[g, 0:rows, :] = (x * cq + pltpu.roll(x, HEAD_DIM // 2, 1) * sq).astype(BF16)
            x = k_ref[:, at].astype(F32)
            o_ref[g, rows : 2 * rows, :] = (x * c + pltpu.roll(x, HEAD_DIM // 2, 1) * s).astype(BF16)
            o_ref[g, 2 * rows :, :] = v_ref[:, at]

    column = pl.BlockSpec((rows, group * HEAD_DIM), lambda i: (0, i))
    whole = pl.BlockSpec((rows, HEAD_DIM), lambda i: (0, 0))
    return pl.pallas_call(
        kernel,
        out_shape=jax.ShapeDtypeStruct((HEADS, 3 * rows, HEAD_DIM), BF16),
        grid=(HEADS // group,),
        in_specs=[column, column, column, whole, whole],
        out_specs=pl.BlockSpec((group, 3 * rows, HEAD_DIM), lambda i: (i, 0, 0)),
        name="prepare",
    )(q, k, v, cosines, sines)


def attend(blocks, scale):
    sources, three_rows, _ = blocks.shape
    rows = three_rows // 3
    length = sources * rows
    bq, kc, kt = 512, 512, 256
    steps = length // bq

    def kernel(scale_ref, b_ref, o_ref, q_ref, k_ref, v_ref, s_ref, m_ref):
        for j in range(sources):
            at = slice(j * rows, (j + 1) * rows)
            q_ref[at, :] = b_ref[j, 0:rows, :]
            k_ref[at, :] = b_ref[j, rows : 2 * rows, :]
            v_ref[at, 0:HEAD_DIM] = b_ref[j, 2 * rows :, :]
        v_ref[:, HEAD_DIM:] = jnp.ones((length, HEAD_DIM), BF16)

        def scores(i, slot):
            q = q_ref[pl.ds(pl.multiple_of(i * bq, bq), bq), :]
            top = None
            for j in range(length // kt):
                s = lax.dot_general(
                    q, k_ref[j * kt : (j + 1) * kt, :], NT, preferred_element_type=F32
                )
                s_ref[slot, :, j * kt : (j + 1) * kt] = s
                for half in range(kt // 128):
                    part = s[:, half * 128 : (half + 1) * 128]
                    top = part if top is None else jnp.maximum(top, part)
            m_ref[slot] = jnp.broadcast_to(jnp.max(top, axis=1, keepdims=True), (bq, 128))

        def mix(i, slot):
            top = jnp.concatenate([m_ref[slot]] * (kc // 128), axis=1)
            total = None
            for j in range(length // kc):
                p = jnp.exp2(s_ref[slot, :, j * kc : (j + 1) * kc] - top).astype(BF16)
                part = jnp.dot(p, v_ref[j * kc : (j + 1) * kc, :], preferred_element_type=F32)
                total = part if total is None else total + part
            out = total[:, :HEAD_DIM] * (scale_ref[0] / total[:, HEAD_DIM:])
            o_ref[pl.ds(pl.multiple_of(i * bq, bq), bq), :] = out.astype(BF16)

        scores(0, 0)

        def pair(t, carry):
            i = 2 * t
            scores(i + 1, 1)
            mix(i, 0)
            scores(i + 2, 0)
            mix(i + 1, 1)
            return carry

        lax.fori_loop(0, (steps - 2) // 2, pair, 0)
        scores(steps - 1, 1)
        mix(steps - 2, 0)
        mix(steps - 1, 1)

    return pl.pallas_call(
        kernel,
        out_shape=jax.ShapeDtypeStruct((length, HEAD_DIM), BF16),
        in_specs=[
            pl.BlockSpec(memory_space=pltpu.SMEM),
            pl.BlockSpec(memory_space=pltpu.VMEM),
        ],
        out_specs=pl.BlockSpec(memory_space=pltpu.VMEM),
        scratch_shapes=[
            pltpu.VMEM((length, HEAD_DIM), BF16),
            pltpu.VMEM((length, HEAD_DIM), BF16),
            pltpu.VMEM((length, 2 * HEAD_DIM), BF16),
            pltpu.VMEM((2, bq, length), F32),
            pltpu.VMEM((2, bq, 128), F32),
        ],
        compiler_params=pltpu.CompilerParams(vmem_limit_bytes=48 << 20),
        name="attend",
    )(scale, blocks)


def exchange(x, partner):
    count = math.prod(lax.axis_size(name) for name in SEQ + BRANCH)
    return lax.ppermute(x, SEQ + BRANCH, [(i, partner(i)) for i in range(count)])


def sum_pieces(pieces, core):
    _, share, _ = pieces.shape

    def kernel(core_ref, p_ref, keep_ref, send_ref):
        for out, part in ((keep_ref, core_ref[0]), (send_ref, 1 - core_ref[0])):
            for block in range(2):
                for r in range(4):
                    head = (2 * block + part) * 4 + r
                    total = jnp.sum(p_ref[pl.ds(head * 4, 4)].astype(F32), axis=0)
                    at = (block * 4 + r) * HEAD_DIM
                    out[:, at : at + HEAD_DIM] = total.astype(BF16)

    shape = jax.ShapeDtypeStruct((share, HEADS // 2 * HEAD_DIM), BF16)
    return pl.pallas_call(
        kernel,
        out_shape=(shape, shape),
        in_specs=[
            pl.BlockSpec(memory_space=pltpu.SMEM),
            pl.BlockSpec(memory_space=pltpu.VMEM),
        ],
        out_specs=(pl.BlockSpec(memory_space=pltpu.VMEM),) * 2,
        name="sum_pieces",
    )(core, pieces)


def weight_block(place_ref, outer, inner):
    core, x, y = place_ref[0], place_ref[1], place_ref[2]
    first = core == 0
    x_there = x ^ jnp.where(first, outer, inner)
    y_there = y ^ jnp.where(first, inner, outer)
    return x_there % 2, y_there * 2 + x_there // 2


def project(place, keep, received, weights):
    share, rows = keep.shape
    _, columns, features = weights[0].shape

    def kernel(place_ref, keep_ref, received_ref, w0, w1, w2, w3, own_ref, send_ref, m_ref, a_ref):
        m_ref[0:share, :] = keep_ref[...]
        m_ref[share:, :] = received_ref[...]
        a_ref[...] = jnp.zeros_like(a_ref)
        for outer, w_ref in enumerate((w0, w1, w2, w3)):
            for inner in range(4):
                row, column = weight_block(place_ref, outer, inner)
                m = m_ref[:, pl.ds(pl.multiple_of(row * features, features), features)]
                at = pl.ds(pl.multiple_of(column * columns, columns), columns)
                a_ref[:, at] += lax.dot_general(
                    m, w_ref[inner], NT, preferred_element_type=F32
                )
        own_ref[...] = a_ref[0:share, :]
        send_ref[...] = a_ref[share:, :].astype(BF16)

    return pl.pallas_call(
        kernel,
        out_shape=(
            jax.ShapeDtypeStruct((share, 8 * columns), F32),
            jax.ShapeDtypeStruct((share, 8 * columns), BF16),
        ),
        in_specs=[pl.BlockSpec(memory_space=pltpu.SMEM)]
        + [pl.BlockSpec(memory_space=pltpu.VMEM)] * 6,
        out_specs=(pl.BlockSpec(memory_space=pltpu.VMEM),) * 2,
        scratch_shapes=[
            pltpu.VMEM((2 * share, rows), BF16),
            pltpu.VMEM((2 * share, 8 * columns), F32),
        ],
        compiler_params=pltpu.CompilerParams(vmem_limit_bytes=32 << 20),
        name="project",
    )(place, keep, received, *weights)


def normalize(own, received, frozen, upstream, gain):
    share, width = own.shape

    def kernel(own_ref, received_ref, frozen_ref, upstream_ref, gain_ref, normed_ref, grad_ref):
        hidden = own_ref[...] + received_ref[...].astype(F32) + frozen_ref[...].astype(F32)
        gain = gain_ref[...]
        up = upstream_ref[...].astype(F32) * gain
        inverse = lax.rsqrt(jnp.mean(hidden * hidden, axis=-1, keepdims=True) + EPS)
        inner = jnp.mean(up * hidden, axis=-1, keepdims=True)
        normed_ref[...] = (hidden * inverse * gain).astype(BF16)
        grad_ref[...] = (
            inverse * up - hidden * (inverse * inverse * inverse) * inner
        ).astype(BF16)

    shape = jax.ShapeDtypeStruct((share, width), BF16)
    return pl.pallas_call(
        kernel,
        out_shape=(shape, shape),
        in_specs=[pl.BlockSpec(memory_space=pltpu.VMEM)] * 5,
        out_specs=(pl.BlockSpec(memory_space=pltpu.VMEM),) * 2,
        name="normalize",
    )(own, received, frozen, upstream, gain)


def project_back(place, grad, received, weights):
    share, width = grad.shape
    _, columns, features = weights[0].shape

    def kernel(place_ref, grad_ref, received_ref, w0, w1, w2, w3, o_ref, g_ref, a_ref):
        core = place_ref[0]
        g_ref[pl.ds(pl.multiple_of(core * share, share), share), :] = grad_ref[...]
        g_ref[pl.ds(pl.multiple_of((1 - core) * share, share), share), :] = received_ref[...]
        a_ref[...] = jnp.zeros_like(a_ref)
        for outer, w_ref in enumerate((w0, w1, w2, w3)):
            for inner in range(4):
                row, column = weight_block(place_ref, outer, inner)
                g = g_ref[:, pl.ds(pl.multiple_of(column * columns, columns), columns)]
                a_ref[row] += jnp.dot(g, w_ref[inner], preferred_element_type=F32)
        for row in range(2):
            o_ref[:, row * features : (row + 1) * features] = a_ref[row].astype(BF16)

    return pl.pallas_call(
        kernel,
        out_shape=jax.ShapeDtypeStruct((2 * share, 2 * features), BF16),
        in_specs=[pl.BlockSpec(memory_space=pltpu.SMEM)]
        + [pl.BlockSpec(memory_space=pltpu.VMEM)] * 6,
        out_specs=pl.BlockSpec(memory_space=pltpu.VMEM),
        scratch_shapes=[
            pltpu.VMEM((2 * share, width), BF16),
            pltpu.VMEM((2, 2 * share, features), F32),
        ],
        compiler_params=pltpu.CompilerParams(vmem_limit_bytes=32 << 20),
        name="project_back",
    )(place, grad, received, *weights)


def scatter_scaled(parts, scale):
    _, tokens, rows = parts.shape
    features = rows // 2

    def kernel(scale_ref, p_ref, o_ref):
        for l in range(2):
            for k in range(2):
                for row in range(2):
                    at = (2 * row + k) * features
                    part = p_ref[2 * l + k, :, row * features : (row + 1) * features]
                    o_ref[l * tokens : (l + 1) * tokens, at : at + features] = (
                        scale_ref[0] * part.astype(F32)
                    ).astype(BF16)

    return pl.pallas_call(
        kernel,
        out_shape=jax.ShapeDtypeStruct((2 * tokens, 2 * rows), BF16),
        in_specs=[
            pl.BlockSpec(memory_space=pltpu.SMEM),
            pl.BlockSpec(memory_space=pltpu.VMEM),
        ],
        out_specs=pl.BlockSpec(memory_space=pltpu.VMEM),
        name="scatter_scaled",
    )(scale, parts)


def on_device(
    q_ctl, k_ctl, v_ctl, positions, branch_ids, cond_scale, out_weight, frozen, norm_gain, cotangent
):
    branch, core = lax.axis_index(BRANCH), lax.axis_index("k")
    z, y, x = lax.axis_index(("c", "z")), lax.axis_index("y"), lax.axis_index(("h", "l"))
    share, _ = frozen.shape
    features, own = out_weight.shape
    place = jnp.stack([core, x, y]).astype(jnp.int32)
    scale = jnp.sum(
        jnp.where(jnp.arange(cond_scale.shape[0]) == branch_ids[0], cond_scale, 0.0)
    ).reshape(1)

    def to_partner(v):
        return exchange(v, lambda i: i ^ 1)

    w = out_weight.T
    for stage in range(4):
        bit = 3 - stage
        other = exchange(w, lambda i: i ^ (32 << bit))
        mine_high = (z >> bit) & 1 == 1
        w = jnp.stack(
            [jnp.where(mine_high, other, w), jnp.where(mine_high, w, other)], axis=stage
        )
    w = w.reshape(16 * own, features)
    w = jnp.stack(
        [w]
        + [exchange(w, lambda i: i ^ (r << (3 if i % 2 == 0 else 1))) for r in range(1, 4)]
    )
    weights = [w] + [
        exchange(w, lambda i: i ^ (r << (1 if i % 2 == 0 else 3))) for r in range(1, 4)
    ]

    def columns_first(v):
        v = v.reshape(v.shape[0], 16, 8, own)
        return jnp.transpose(v, (0, 2, 1, 3)).reshape(v.shape[0], -1)

    def columns_back(v):
        v = v.reshape(v.shape[0], 8, 16, own)
        return jnp.transpose(v, (0, 2, 1, 3)).reshape(v.shape[0], -1)

    frozen = columns_first(frozen)
    gain = columns_first(norm_gain[None])
    upstream = columns_first(lax.dynamic_slice_in_dim(cotangent, branch * share, share, 0))

    cosines, sines = rope_tables(positions)
    blocks = prepare(q_ctl[0], k_ctl[0], v_ctl[0], cosines, sines)
    blocks = lax.all_to_all(blocks, CLIP, 0, 0, tiled=True)
    blocks, frozen, gain, upstream = lax.optimization_barrier((blocks, frozen, gain, upstream))
    attended = attend(blocks, scale)
    pieces = lax.all_to_all(
        attended.reshape(HEADS * 4, share, HEAD_DIM), CLIP + BRANCH, 0, 0, tiled=True
    )
    keep, send = sum_pieces(pieces, core.reshape(1))
    own_part, send = project(place, keep, to_partner(send), weights)
    normed, grad = normalize(own_part, to_partner(send), frozen, upstream, gain)
    cot = project_back(place, grad, to_partner(grad), weights)
    parts = lax.all_gather(cot, BRANCH, axis=0, tiled=False)
    grad_attn = scatter_scaled(parts, scale)
    return columns_back(normed), grad_attn[None]


def solution(mesh):
    fine = Mesh(mesh.devices.reshape(8, 2, 4, 2, 2, 2), SEQ + BRANCH)

    return jax.shard_map(
        on_device,
        mesh=fine,
        in_specs=(
            P(BRANCH, SEQ, None),
            P(BRANCH, SEQ, None),
            P(BRANCH, SEQ, None),
            P(SEQ),
            P(BRANCH),
            P(),
            P(BRANCH, SEQ),
            P(SEQ + BRANCH, None),
            P(),
            P(SEQ, None),
        ),
        out_specs=(P(SEQ + BRANCH, None), P(BRANCH, SEQ, None)),
        check_vma=False,
    )
```

```python
import math

import jax
import jax.numpy as jnp
from jax import lax
from jax.experimental import pallas as pl
from jax.experimental.pallas import tpu as pltpu
from jax.sharding import Mesh
from jax.sharding import PartitionSpec as P


HEADS = 16
HEAD_DIM = 128
EPS = 1e-06
CLIP = ("z", "y", "h")
SEQ = ("c", "z", "y", "h")
BRANCH = ("l", "k")
F32 = jnp.float32
BF16 = jnp.bfloat16
NT = (((1,), (1,)), ((), ()))


def rope_tables(positions):
    exponents = jnp.arange(HEAD_DIM // 2, dtype=F32) * (2.0 / HEAD_DIM)
    angles = positions.astype(F32)[:, None] * (10000.0 ** (-exponents))
    cosines, sines = jnp.cos(angles), jnp.sin(angles)
    return (
        jnp.concatenate([cosines, cosines], axis=1),
        jnp.concatenate([-sines, sines], axis=1),
    )


def prepare(q, k, v, cosines, sines):
    rows = q.shape[0]
    factor = math.log2(math.e) / math.sqrt(HEAD_DIM)
    group = 4

    def kernel(q_ref, k_ref, v_ref, c_ref, s_ref, o_ref):
        c, s = c_ref[...], s_ref[...]
        cq, sq = c * factor, s * factor
        for g in range(group):
            at = slice(g * HEAD_DIM, (g + 1) * HEAD_DIM)
            x = q_ref[:, at].astype(F32)
            o_ref[g, 0:rows, :] = (x * cq + pltpu.roll(x, HEAD_DIM // 2, 1) * sq).astype(BF16)
            x = k_ref[:, at].astype(F32)
            o_ref[g, rows : 2 * rows, :] = (x * c + pltpu.roll(x, HEAD_DIM // 2, 1) * s).astype(BF16)
            o_ref[g, 2 * rows :, :] = v_ref[:, at]

    column = pl.BlockSpec((rows, group * HEAD_DIM), lambda i: (0, i))
    whole = pl.BlockSpec((rows, HEAD_DIM), lambda i: (0, 0))
    return pl.pallas_call(
        kernel,
        out_shape=jax.ShapeDtypeStruct((HEADS, 3 * rows, HEAD_DIM), BF16),
        grid=(HEADS // group,),
        in_specs=[column, column, column, whole, whole],
        out_specs=pl.BlockSpec((group, 3 * rows, HEAD_DIM), lambda i: (i, 0, 0)),
        name="prepare",
    )(q, k, v, cosines, sines)


def attend(blocks, scale, part, received=None):
    sources, three_rows, _ = blocks.shape
    rows = three_rows // 3
    length = sources * rows
    share = rows // 4
    queries = length // 2
    bq, kc, kt = 384, 512, 256
    steps = queries // bq

    def kernel(part_ref, scale_ref, b_ref, *refs):
        refs = list(refs)
        r_ref = refs.pop(0) if received is not None else None
        o_ref, q_ref, k_ref, v_ref, s_ref, m_ref = refs
        for j in range(sources):
            at = slice(j * rows, (j + 1) * rows)
            for l in range(2):
                first = pl.multiple_of((2 * l + part_ref[0]) * share, share)
                to = (2 * j + l) * share
                q_ref[to : to + share, :] = b_ref[j, pl.ds(first, share), :]
            k_ref[at, :] = b_ref[j, rows : 2 * rows, :]
            v_ref[at, 0:HEAD_DIM] = b_ref[j, 2 * rows :, :]
        v_ref[:, HEAD_DIM:] = jnp.ones((length, HEAD_DIM), BF16)

        def scores(i, slot):
            q = q_ref[pl.ds(pl.multiple_of(i * bq, bq), bq), :]
            top = None
            for j in range(length // kt):
                s = lax.dot_general(
                    q, k_ref[j * kt : (j + 1) * kt, :], NT, preferred_element_type=F32
                )
                s_ref[slot, :, j * kt : (j + 1) * kt] = s
                for half in range(kt // 128):
                    piece = s[:, half * 128 : (half + 1) * 128]
                    top = piece if top is None else jnp.maximum(top, piece)
            m_ref[slot] = jnp.broadcast_to(jnp.max(top, axis=1, keepdims=True), (bq, 128))

        def mix(i, slot):
            top = jnp.concatenate([m_ref[slot]] * (kc // 128), axis=1)
            total = None
            for j in range(length // kc):
                p = jnp.exp2(s_ref[slot, :, j * kc : (j + 1) * kc] - top).astype(BF16)
                piece = jnp.dot(p, v_ref[j * kc : (j + 1) * kc, :], preferred_element_type=F32)
                total = piece if total is None else total + piece
            out = total[:, :HEAD_DIM] * (scale_ref[0] / total[:, HEAD_DIM:])
            at = pl.ds(pl.multiple_of(i * bq, bq), bq)
            if r_ref is not None:
                out = out + r_ref[at, :].astype(F32)
            o_ref[at, :] = out.astype(BF16)

        scores(0, 0)

        def pair(t, carry):
            i = 2 * t
            scores(i + 1, 1)
            mix(i, 0)
            scores(i + 2, 0)
            mix(i + 1, 1)
            return carry

        lax.fori_loop(0, (steps - 2) // 2, pair, 0)
        scores(steps - 1, 1)
        mix(steps - 2, 0)
        mix(steps - 1, 1)

    extra = () if received is None else (received,)
    return pl.pallas_call(
        kernel,
        out_shape=jax.ShapeDtypeStruct((queries, HEAD_DIM), BF16),
        in_specs=[pl.BlockSpec(memory_space=pltpu.SMEM)] * 2
        + [pl.BlockSpec(memory_space=pltpu.VMEM)] * (1 + len(extra)),
        out_specs=pl.BlockSpec(memory_space=pltpu.VMEM),
        scratch_shapes=[
            pltpu.VMEM((queries, HEAD_DIM), BF16),
            pltpu.VMEM((length, HEAD_DIM), BF16),
            pltpu.VMEM((length, 2 * HEAD_DIM), BF16),
            pltpu.VMEM((2, bq, length), F32),
            pltpu.VMEM((2, bq, 128), F32),
        ],
        compiler_params=pltpu.CompilerParams(vmem_limit_bytes=40 << 20),
        cost_estimate=pl.CostEstimate(
            flops=4 * queries * length * HEAD_DIM,
            bytes_accessed=2 * blocks.size,
            transcendentals=queries * length,
        ),
        name="attend_last" if extra else "attend_first",
    )(part, scale, blocks, *extra)


def order_along_z(w, z):
    def kernel(z_ref, w_ref, o_ref):
        for other in range(16):
            d = z_ref[0] ^ other
            at = (d & 1) * 8 + ((d >> 1) & 1) * 4 + ((d >> 2) & 1) * 2 + ((d >> 3) & 1)
            o_ref[other] = w_ref[at]

    return pl.pallas_call(
        kernel,
        out_shape=jax.ShapeDtypeStruct(w.shape, BF16),
        in_specs=[
            pl.BlockSpec(memory_space=pltpu.SMEM),
            pl.BlockSpec(memory_space=pltpu.VMEM),
        ],
        out_specs=pl.BlockSpec(memory_space=pltpu.VMEM),
        name="order_along_z",
    )(z, w)


def exchange(x, partner):
    count = math.prod(lax.axis_size(name) for name in SEQ + BRANCH)
    return lax.ppermute(x, SEQ + BRANCH, [(i, partner(i)) for i in range(count)])


def sum_pieces(pieces, core):
    _, share, _ = pieces.shape

    def kernel(core_ref, p_ref, keep_ref, send_ref):
        for out, part in ((keep_ref, core_ref[0]), (send_ref, 1 - core_ref[0])):
            for block in range(2):
                for r in range(4):
                    head = (2 * block + part) * 4 + r
                    total = p_ref[2 * head].astype(F32) + p_ref[2 * head + 1].astype(F32)
                    at = (block * 4 + r) * HEAD_DIM
                    out[:, at : at + HEAD_DIM] = total.astype(BF16)

    shape = jax.ShapeDtypeStruct((share, HEADS // 2 * HEAD_DIM), BF16)
    return pl.pallas_call(
        kernel,
        out_shape=(shape, shape),
        in_specs=[
            pl.BlockSpec(memory_space=pltpu.SMEM),
            pl.BlockSpec(memory_space=pltpu.VMEM),
        ],
        out_specs=(pl.BlockSpec(memory_space=pltpu.VMEM),) * 2,
        name="sum_pieces",
    )(core, pieces)


def weight_block(place_ref, outer, inner):
    core, x, y = place_ref[0], place_ref[1], place_ref[2]
    first = core == 0
    x_there = x ^ jnp.where(first, outer, inner)
    y_there = y ^ jnp.where(first, inner, outer)
    return x_there % 2, y_there * 2 + x_there // 2


def project(place, keep, received, weights):
    share, rows = keep.shape
    _, columns, features = weights[0].shape

    def kernel(place_ref, keep_ref, received_ref, w0, w1, w2, w3, own_ref, send_ref, m_ref, a_ref):
        m_ref[0:share, :] = keep_ref[...]
        m_ref[share:, :] = received_ref[...]
        a_ref[...] = jnp.zeros_like(a_ref)
        for outer, w_ref in enumerate((w0, w1, w2, w3)):
            for inner in range(4):
                row, column = weight_block(place_ref, outer, inner)
                m = m_ref[:, pl.ds(pl.multiple_of(row * features, features), features)]
                at = pl.ds(pl.multiple_of(column * columns, columns), columns)
                a_ref[:, at] += lax.dot_general(
                    m, w_ref[inner], NT, preferred_element_type=F32
                )
        own_ref[...] = a_ref[0:share, :]
        send_ref[...] = a_ref[share:, :].astype(BF16)

    return pl.pallas_call(
        kernel,
        out_shape=(
            jax.ShapeDtypeStruct((share, 8 * columns), F32),
            jax.ShapeDtypeStruct((share, 8 * columns), BF16),
        ),
        in_specs=[pl.BlockSpec(memory_space=pltpu.SMEM)]
        + [pl.BlockSpec(memory_space=pltpu.VMEM)] * 6,
        out_specs=(pl.BlockSpec(memory_space=pltpu.VMEM),) * 2,
        scratch_shapes=[
            pltpu.VMEM((2 * share, rows), BF16),
            pltpu.VMEM((2 * share, 8 * columns), F32),
        ],
        compiler_params=pltpu.CompilerParams(vmem_limit_bytes=32 << 20),
        name="project",
    )(place, keep, received, *weights)


def widen(frozen, upstream, gain):
    def kernel(frozen_ref, upstream_ref, gain_ref, f_ref, u_ref):
        f_ref[...] = frozen_ref[...].astype(F32)
        u_ref[...] = upstream_ref[...].astype(F32) * gain_ref[...]

    shape = jax.ShapeDtypeStruct(frozen.shape, F32)
    return pl.pallas_call(
        kernel,
        out_shape=(shape, shape),
        in_specs=[pl.BlockSpec(memory_space=pltpu.VMEM)] * 3,
        out_specs=(pl.BlockSpec(memory_space=pltpu.VMEM),) * 2,
        name="widen",
    )(frozen, upstream, gain)


def normalize(own, received, frozen, upstream, gain, block):
    share, width = own.shape

    def kernel(own_ref, received_ref, frozen_ref, up_ref, gain_ref, normed_ref, grad_ref, n_ref):
        hidden = own_ref[...] + received_ref[...].astype(F32) + frozen_ref[...]
        up = up_ref[...]
        inverse = lax.rsqrt(jnp.mean(hidden * hidden, axis=-1, keepdims=True) + EPS)
        inner = jnp.mean(up * hidden, axis=-1, keepdims=True)
        grad_ref[...] = (
            inverse * up - hidden * (inverse * inverse * inverse) * inner
        ).astype(BF16)
        normed = hidden * inverse * gain_ref[...]
        for z in range(16):
            for group in range(8):
                to, at = (z * 8 + group) * block, (group * 16 + z) * block
                n_ref[:, to : to + block] = normed[:, at : at + block]
        normed_ref[...] = n_ref[...].astype(BF16)

    shape = jax.ShapeDtypeStruct((share, width), BF16)
    return pl.pallas_call(
        kernel,
        out_shape=(shape, shape),
        in_specs=[pl.BlockSpec(memory_space=pltpu.VMEM)] * 5,
        out_specs=(pl.BlockSpec(memory_space=pltpu.VMEM),) * 2,
        scratch_shapes=[pltpu.VMEM((share, width), F32)],
        name="normalize",
    )(own, received, frozen, upstream, gain)


def project_back(place, grad, received, weights):
    share, width = grad.shape
    _, columns, features = weights[0].shape

    def kernel(place_ref, grad_ref, received_ref, w0, w1, w2, w3, o_ref, g_ref, a_ref):
        core = place_ref[0]
        g_ref[pl.ds(pl.multiple_of(core * share, share), share), :] = grad_ref[...]
        g_ref[pl.ds(pl.multiple_of((1 - core) * share, share), share), :] = received_ref[...]
        a_ref[...] = jnp.zeros_like(a_ref)
        for outer, w_ref in enumerate((w0, w1, w2, w3)):
            for inner in range(4):
                row, column = weight_block(place_ref, outer, inner)
                g = g_ref[:, pl.ds(pl.multiple_of(column * columns, columns), columns)]
                a_ref[row] += jnp.dot(g, w_ref[inner], preferred_element_type=F32)
        for row in range(2):
            o_ref[:, row * features : (row + 1) * features] = a_ref[row].astype(BF16)

    return pl.pallas_call(
        kernel,
        out_shape=jax.ShapeDtypeStruct((2 * share, 2 * features), BF16),
        in_specs=[pl.BlockSpec(memory_space=pltpu.SMEM)]
        + [pl.BlockSpec(memory_space=pltpu.VMEM)] * 6,
        out_specs=pl.BlockSpec(memory_space=pltpu.VMEM),
        scratch_shapes=[
            pltpu.VMEM((2 * share, width), BF16),
            pltpu.VMEM((2, 2 * share, features), F32),
        ],
        compiler_params=pltpu.CompilerParams(vmem_limit_bytes=32 << 20),
        name="project_back",
    )(place, grad, received, *weights)


def scatter_scaled(parts, scale):
    _, tokens, rows = parts.shape
    features = rows // 2

    def kernel(scale_ref, p_ref, o_ref):
        for l in range(2):
            for k in range(2):
                for row in range(2):
                    at = (2 * row + k) * features
                    part = p_ref[2 * l + k, :, row * features : (row + 1) * features]
                    o_ref[l * tokens : (l + 1) * tokens, at : at + features] = (
                        scale_ref[0] * part.astype(F32)
                    ).astype(BF16)

    return pl.pallas_call(
        kernel,
        out_shape=jax.ShapeDtypeStruct((2 * tokens, 2 * rows), BF16),
        in_specs=[
            pl.BlockSpec(memory_space=pltpu.SMEM),
            pl.BlockSpec(memory_space=pltpu.VMEM),
        ],
        out_specs=pl.BlockSpec(memory_space=pltpu.VMEM),
        name="scatter_scaled",
    )(scale, parts)


def on_device(
    q_ctl, k_ctl, v_ctl, positions, branch_ids, cond_scale, out_weight, frozen, norm_gain, cotangent
):
    branch, core = lax.axis_index(BRANCH), lax.axis_index("k")
    z, y, x = lax.axis_index(("c", "z")), lax.axis_index("y"), lax.axis_index(("h", "l"))
    share, _ = frozen.shape
    features, own = out_weight.shape
    place = jnp.stack([core, x, y]).astype(jnp.int32)
    scale = jnp.sum(
        jnp.where(jnp.arange(cond_scale.shape[0]) == branch_ids[0], cond_scale, 0.0)
    ).reshape(1)

    def to_partner(v):
        return exchange(v, lambda i: i ^ 1)

    w = out_weight.T[None]
    for stage in range(4):
        w = jnp.concatenate([w, exchange(w, lambda i: i ^ (256 >> stage))])
    w = order_along_z(w, z.astype(jnp.int32).reshape(1)).reshape(16 * own, features)
    w = jnp.stack(
        [w]
        + [exchange(w, lambda i: i ^ (r << (3 if i % 2 == 0 else 1))) for r in range(1, 4)]
    )
    weights = [w] + [
        exchange(w, lambda i: i ^ (r << (1 if i % 2 == 0 else 3))) for r in range(1, 4)
    ]

    def columns_first(v):
        v = v.reshape(v.shape[0], 16, 8, own)
        return jnp.transpose(v, (0, 2, 1, 3)).reshape(v.shape[0], -1)

    gain = columns_first(norm_gain[None])
    upstream = columns_first(lax.dynamic_slice_in_dim(cotangent, branch * share, share, 0))
    frozen, upstream = widen(columns_first(frozen), upstream, gain)

    cosines, sines = rope_tables(positions)
    blocks = prepare(q_ctl[0], k_ctl[0], v_ctl[0], cosines, sines)
    blocks = lax.all_to_all(blocks, CLIP, 0, 0, tiled=True)
    blocks, frozen, upstream, gain = lax.optimization_barrier((blocks, frozen, upstream, gain))
    core = core.astype(jnp.int32).reshape(1)
    received = to_partner(attend(blocks, scale, 1 - core))
    attended = attend(blocks, scale, core, received)
    pieces = lax.all_to_all(
        attended.reshape(HEADS * 2, share, HEAD_DIM), CLIP + ("l",), 0, 0, tiled=True
    )
    keep, send = sum_pieces(pieces, core)
    own_part, send = project(place, keep, to_partner(send), weights)
    normed, grad = normalize(own_part, to_partner(send), frozen, upstream, gain, own)
    cot = project_back(place, grad, to_partner(grad), weights)
    parts = lax.all_gather(cot, BRANCH, axis=0, tiled=False)
    grad_attn = scatter_scaled(parts, scale)
    return normed, grad_attn[None]


def solution(mesh):
    fine = Mesh(mesh.devices.reshape(8, 2, 4, 2, 2, 2), SEQ + BRANCH)

    return jax.shard_map(
        on_device,
        mesh=fine,
        in_specs=(
            P(BRANCH, SEQ, None),
            P(BRANCH, SEQ, None),
            P(BRANCH, SEQ, None),
            P(SEQ),
            P(BRANCH),
            P(),
            P(BRANCH, SEQ),
            P(SEQ + BRANCH, None),
            P(),
            P(SEQ, None),
        ),
        out_specs=(P(SEQ + BRANCH, None), P(BRANCH, SEQ, None)),
        check_vma=False,
    )
```

```python
import math

import jax
import jax.numpy as jnp
from jax import lax
from jax.experimental import pallas as pl
from jax.experimental.pallas import tpu as pltpu
from jax.sharding import Mesh
from jax.sharding import PartitionSpec as P


HEADS = 16
HEAD_DIM = 128
EPS = 1e-06
CLIP = ("z", "y", "h")
SEQ = ("c", "z", "y", "h")
BRANCH = ("l", "k")
F32 = jnp.float32
BF16 = jnp.bfloat16
NT = (((1,), (1,)), ((), ()))


def rope_tables(positions):
    exponents = jnp.arange(HEAD_DIM // 2, dtype=F32) * (2.0 / HEAD_DIM)
    angles = positions.astype(F32)[:, None] * (10000.0 ** (-exponents))
    cosines, sines = jnp.cos(angles), jnp.sin(angles)
    return (
        jnp.concatenate([cosines, cosines], axis=1),
        jnp.concatenate([-sines, sines], axis=1),
    )


def prepare(q, k, v, cosines, sines):
    rows = q.shape[0]
    factor = math.log2(math.e) / math.sqrt(HEAD_DIM)
    group = 4

    def kernel(q_ref, k_ref, v_ref, c_ref, s_ref, o_ref):
        c, s = c_ref[...], s_ref[...]
        cq, sq = c * factor, s * factor
        for g in range(group):
            at = slice(g * HEAD_DIM, (g + 1) * HEAD_DIM)
            x = q_ref[:, at].astype(F32)
            o_ref[g, 0:rows, :] = (x * cq + pltpu.roll(x, HEAD_DIM // 2, 1) * sq).astype(BF16)
            x = k_ref[:, at].astype(F32)
            o_ref[g, rows : 2 * rows, :] = (x * c + pltpu.roll(x, HEAD_DIM // 2, 1) * s).astype(BF16)
            o_ref[g, 2 * rows :, :] = v_ref[:, at]

    column = pl.BlockSpec((rows, group * HEAD_DIM), lambda i: (0, i))
    whole = pl.BlockSpec((rows, HEAD_DIM), lambda i: (0, 0))
    return pl.pallas_call(
        kernel,
        out_shape=jax.ShapeDtypeStruct((HEADS, 3 * rows, HEAD_DIM), BF16),
        grid=(HEADS // group,),
        in_specs=[column, column, column, whole, whole],
        out_specs=pl.BlockSpec((group, 3 * rows, HEAD_DIM), lambda i: (i, 0, 0)),
        name="prepare",
    )(q, k, v, cosines, sines)


def attend(blocks, scale, part, received=None):
    sources, three_rows, _ = blocks.shape
    rows = three_rows // 3
    length = sources * rows
    share = rows // 4
    queries = length // 2
    bq, kc, kt = 384, 512, 256
    steps = queries // bq

    def kernel(part_ref, scale_ref, b_ref, *refs):
        refs = list(refs)
        r_ref = refs.pop(0) if received is not None else None
        o_ref, q_ref, k_ref, v_ref, s_ref, m_ref = refs
        for j in range(sources):
            at = slice(j * rows, (j + 1) * rows)
            for l in range(2):
                first = pl.multiple_of((2 * l + part_ref[0]) * share, share)
                to = (2 * j + l) * share
                q_ref[to : to + share, :] = b_ref[j, pl.ds(first, share), :]
            k_ref[at, :] = b_ref[j, rows : 2 * rows, :]
            v_ref[at, 0:HEAD_DIM] = b_ref[j, 2 * rows :, :]
        v_ref[:, HEAD_DIM:] = jnp.ones((length, HEAD_DIM), BF16)

        def scores(i, slot):
            q = q_ref[pl.ds(pl.multiple_of(i * bq, bq), bq), :]
            top = None
            for j in range(length // kt):
                s = lax.dot_general(
                    q, k_ref[j * kt : (j + 1) * kt, :], NT, preferred_element_type=F32
                )
                s_ref[slot, :, j * kt : (j + 1) * kt] = s
                for half in range(kt // 128):
                    piece = s[:, half * 128 : (half + 1) * 128]
                    top = piece if top is None else jnp.maximum(top, piece)
            m_ref[slot] = jnp.broadcast_to(jnp.max(top, axis=1, keepdims=True), (bq, 128))

        def mix(i, slot):
            top = jnp.concatenate([m_ref[slot]] * (kc // 128), axis=1)
            total = None
            for j in range(length // kc):
                p = jnp.exp2(s_ref[slot, :, j * kc : (j + 1) * kc] - top).astype(BF16)
                piece = jnp.dot(p, v_ref[j * kc : (j + 1) * kc, :], preferred_element_type=F32)
                total = piece if total is None else total + piece
            out = total[:, :HEAD_DIM] * (scale_ref[0] / total[:, HEAD_DIM:])
            at = pl.ds(pl.multiple_of(i * bq, bq), bq)
            if r_ref is not None:
                out = out + r_ref[at, :].astype(F32)
            o_ref[at, :] = out.astype(BF16)

        scores(0, 0)

        def pair(t, carry):
            i = 2 * t
            scores(i + 1, 1)
            mix(i, 0)
            scores(i + 2, 0)
            mix(i + 1, 1)
            return carry

        lax.fori_loop(0, (steps - 2) // 2, pair, 0)
        scores(steps - 1, 1)
        mix(steps - 2, 0)
        mix(steps - 1, 1)

    extra = () if received is None else (received,)
    return pl.pallas_call(
        kernel,
        out_shape=jax.ShapeDtypeStruct((queries, HEAD_DIM), BF16),
        in_specs=[pl.BlockSpec(memory_space=pltpu.SMEM)] * 2
        + [pl.BlockSpec(memory_space=pltpu.VMEM)] * (1 + len(extra)),
        out_specs=pl.BlockSpec(memory_space=pltpu.VMEM),
        scratch_shapes=[
            pltpu.VMEM((queries, HEAD_DIM), BF16),
            pltpu.VMEM((length, HEAD_DIM), BF16),
            pltpu.VMEM((length, 2 * HEAD_DIM), BF16),
            pltpu.VMEM((2, bq, length), F32),
            pltpu.VMEM((2, bq, 128), F32),
        ],
        compiler_params=pltpu.CompilerParams(vmem_limit_bytes=40 << 20),
        cost_estimate=pl.CostEstimate(
            flops=4 * queries * length * HEAD_DIM,
            bytes_accessed=2 * blocks.size,
            transcendentals=queries * length,
        ),
        name="attend_last" if extra else "attend_first",
    )(part, scale, blocks, *extra)


def order_along_z(w, place):
    def kernel(place_ref, w_ref, o_ref):
        c, z = place_ref[0], place_ref[1]
        for there in range(16):
            d = (there // 2 - c) * (1 - 2 * z) & 7
            at = (d & 1) * 8 + ((d >> 1) & 1) * 4 + ((d >> 2) & 1) * 2 + ((there & 1) ^ z)
            o_ref[there] = w_ref[at]

    return pl.pallas_call(
        kernel,
        out_shape=jax.ShapeDtypeStruct(w.shape, BF16),
        in_specs=[
            pl.BlockSpec(memory_space=pltpu.SMEM),
            pl.BlockSpec(memory_space=pltpu.VMEM),
        ],
        out_specs=pl.BlockSpec(memory_space=pltpu.VMEM),
        name="order_along_z",
    )(place, w)


def exchange(x, partner):
    count = math.prod(lax.axis_size(name) for name in SEQ + BRANCH)
    return lax.ppermute(x, SEQ + BRANCH, [(i, partner(i)) for i in range(count)])


def sum_pieces(pieces, core):
    _, share, _ = pieces.shape

    def kernel(core_ref, p_ref, keep_ref, send_ref):
        for out, part in ((keep_ref, core_ref[0]), (send_ref, 1 - core_ref[0])):
            for block in range(2):
                for r in range(4):
                    head = (2 * block + part) * 4 + r
                    total = p_ref[2 * head].astype(F32) + p_ref[2 * head + 1].astype(F32)
                    at = (block * 4 + r) * HEAD_DIM
                    out[:, at : at + HEAD_DIM] = total.astype(BF16)

    shape = jax.ShapeDtypeStruct((share, HEADS // 2 * HEAD_DIM), BF16)
    return pl.pallas_call(
        kernel,
        grid=(1,),
        out_shape=(shape, shape),
        in_specs=[
            pl.BlockSpec(memory_space=pltpu.SMEM),
            whole(pieces),
        ],
        out_specs=(whole(shape),) * 2,
        name="sum_pieces",
    )(core, pieces)


def weight_block(place_ref, outer, inner):
    core, x, y = place_ref[0], place_ref[1], place_ref[2]
    first = core == 0
    x_there = x ^ jnp.where(first, outer, inner)
    y_there = y ^ jnp.where(first, inner, outer)
    return x_there % 2, y_there * 2 + x_there // 2


def whole(x):
    return pl.BlockSpec(x.shape, lambda *_: (0,) * len(x.shape))


def project(place, keep, received, weights):
    share, rows = keep.shape
    pieces, columns, features = weights[0].shape
    own = jax.ShapeDtypeStruct((share, 8 * columns), F32)
    send = jax.ShapeDtypeStruct((share, 8 * columns), BF16)

    def kernel(place_ref, keep_ref, received_ref, w0, w1, w2, w3, own_ref, send_ref, m_ref, a_ref):
        inner = pl.program_id(0)

        @pl.when(inner == 0)
        def _():
            m_ref[0:share, :] = keep_ref[...]
            m_ref[share:, :] = received_ref[...]
            a_ref[...] = jnp.zeros_like(a_ref)

        for outer, w_ref in enumerate((w0, w1, w2, w3)):
            row, column = weight_block(place_ref, outer, inner)
            m = m_ref[:, pl.ds(pl.multiple_of(row * features, features), features)]
            at = pl.ds(pl.multiple_of(column * columns, columns), columns)
            a_ref[:, at] += lax.dot_general(m, w_ref[0], NT, preferred_element_type=F32)

        @pl.when(inner == pieces - 1)
        def _():
            own_ref[...] = a_ref[0:share, :]
            send_ref[...] = a_ref[share:, :].astype(BF16)

    piece = pl.BlockSpec((1, columns, features), lambda i: (i, 0, 0))
    return pl.pallas_call(
        kernel,
        out_shape=(own, send),
        grid=(pieces,),
        in_specs=[pl.BlockSpec(memory_space=pltpu.SMEM), whole(keep), whole(received)]
        + [piece] * 4,
        out_specs=(whole(own), whole(send)),
        scratch_shapes=[
            pltpu.VMEM((2 * share, rows), BF16),
            pltpu.VMEM((2 * share, 8 * columns), F32),
        ],
        name="project",
    )(place, keep, received, *weights)


def widen(frozen, upstream, gain):
    def kernel(frozen_ref, upstream_ref, gain_ref, f_ref, u_ref):
        f_ref[...] = frozen_ref[...].astype(F32)
        u_ref[...] = upstream_ref[...].astype(F32) * gain_ref[...]

    shape = jax.ShapeDtypeStruct(frozen.shape, F32)
    return pl.pallas_call(
        kernel,
        out_shape=(shape, shape),
        in_specs=[pl.BlockSpec(memory_space=pltpu.VMEM)] * 3,
        out_specs=(pl.BlockSpec(memory_space=pltpu.VMEM),) * 2,
        name="widen",
    )(frozen, upstream, gain)


def normalize(own, received, frozen, upstream, gain, block):
    share, width = own.shape

    def kernel(own_ref, received_ref, frozen_ref, up_ref, gain_ref, normed_ref, grad_ref, n_ref):
        hidden = own_ref[...] + received_ref[...].astype(F32) + frozen_ref[...]
        up = up_ref[...]
        inverse = lax.rsqrt(jnp.mean(hidden * hidden, axis=-1, keepdims=True) + EPS)
        inner = jnp.mean(up * hidden, axis=-1, keepdims=True)
        grad_ref[...] = (
            inverse * up - hidden * (inverse * inverse * inverse) * inner
        ).astype(BF16)
        normed = hidden * inverse * gain_ref[...]
        for z in range(16):
            for group in range(8):
                to, at = (z * 8 + group) * block, (group * 16 + z) * block
                n_ref[:, to : to + block] = normed[:, at : at + block]
        normed_ref[...] = n_ref[...].astype(BF16)

    shape = jax.ShapeDtypeStruct((share, width), BF16)
    return pl.pallas_call(
        kernel,
        out_shape=(shape, shape),
        grid=(1,),
        in_specs=[whole(v) for v in (own, received, frozen, upstream, gain)],
        out_specs=(whole(shape),) * 2,
        scratch_shapes=[pltpu.VMEM((share, width), F32)],
        name="normalize",
    )(own, received, frozen, upstream, gain)


def project_back(place, grad, received, weights):
    share, width = grad.shape
    pieces, columns, features = weights[0].shape
    out = jax.ShapeDtypeStruct((2 * share, 2 * features), BF16)

    def kernel(place_ref, grad_ref, received_ref, w0, w1, w2, w3, o_ref, g_ref, a_ref):
        inner, core = pl.program_id(0), place_ref[0]

        @pl.when(inner == 0)
        def _():
            g_ref[pl.ds(pl.multiple_of(core * share, share), share), :] = grad_ref[...]
            g_ref[pl.ds(pl.multiple_of((1 - core) * share, share), share), :] = received_ref[...]
            a_ref[...] = jnp.zeros_like(a_ref)

        for outer, w_ref in enumerate((w0, w1, w2, w3)):
            row, column = weight_block(place_ref, outer, inner)
            g = g_ref[:, pl.ds(pl.multiple_of(column * columns, columns), columns)]
            a_ref[row] += jnp.dot(g, w_ref[0], preferred_element_type=F32)

        @pl.when(inner == pieces - 1)
        def _():
            for row in range(2):
                o_ref[:, row * features : (row + 1) * features] = a_ref[row].astype(BF16)

    piece = pl.BlockSpec((1, columns, features), lambda i: (i, 0, 0))
    return pl.pallas_call(
        kernel,
        out_shape=out,
        grid=(pieces,),
        in_specs=[pl.BlockSpec(memory_space=pltpu.SMEM), whole(grad), whole(received)]
        + [piece] * 4,
        out_specs=whole(out),
        scratch_shapes=[
            pltpu.VMEM((2 * share, width), BF16),
            pltpu.VMEM((2, 2 * share, features), F32),
        ],
        name="project_back",
    )(place, grad, received, *weights)


def scatter_scaled(parts, scale):
    _, tokens, rows = parts.shape
    features = rows // 2

    def kernel(scale_ref, p_ref, o_ref):
        for k in range(2):
            for row in range(2):
                at = (2 * row + k) * features
                part = p_ref[k, :, row * features : (row + 1) * features]
                o_ref[:, at : at + features] = (scale_ref[0] * part.astype(F32)).astype(BF16)

    return pl.pallas_call(
        kernel,
        out_shape=jax.ShapeDtypeStruct((2 * tokens, 2 * rows), BF16),
        grid=(2,),
        in_specs=[
            pl.BlockSpec(memory_space=pltpu.SMEM),
            pl.BlockSpec((2, tokens, rows), lambda l: (l, 0, 0)),
        ],
        out_specs=pl.BlockSpec((tokens, 2 * rows), lambda l: (l, 0)),
        name="scatter_scaled",
    )(scale, parts)


def on_device(
    q_ctl, k_ctl, v_ctl, positions, branch_ids, cond_scale, out_weight, frozen, norm_gain, cotangent
):
    branch, core = lax.axis_index(BRANCH), lax.axis_index("k")
    clip, z = lax.axis_index("c"), lax.axis_index("z")
    y, x = lax.axis_index("y"), lax.axis_index(("h", "l"))
    share, _ = frozen.shape
    features, own = out_weight.shape
    place = jnp.stack([core, x, y]).astype(jnp.int32)
    scale = jnp.sum(
        jnp.where(jnp.arange(cond_scale.shape[0]) == branch_ids[0], cond_scale, 0.0)
    ).reshape(1)

    def to_partner(v):
        return exchange(v, lambda i: i ^ 1)

    w = out_weight.T[None]
    w = jnp.concatenate([w, exchange(w, lambda i: i ^ 32)])

    def away(step):
        return lambda i: (i + (step if i & 32 else -step) * 64) % 512

    cosines, sines = rope_tables(positions)
    blocks = prepare(q_ctl[0], k_ctl[0], v_ctl[0], cosines, sines)
    w, blocks = lax.optimization_barrier((w, blocks))
    blocks = lax.all_to_all(blocks, CLIP, 0, 0, tiled=True)
    for step in (4, 2, 1):
        w = jnp.concatenate([w, exchange(w, away(step))])
    w = order_along_z(w, jnp.stack([clip, z]).astype(jnp.int32)).reshape(16 * own, features)
    arrived = [exchange(w, lambda i: i ^ (r << (3 if i % 2 == 0 else 1))) for r in range(1, 4)]
    w = jnp.stack([w] + arrived)
    weights = [w] + [
        exchange(w, lambda i: i ^ (r << (1 if i % 2 == 0 else 3))) for r in range(1, 4)
    ]

    def columns_first(v):
        v = v.reshape(v.shape[0], 16, 8, own)
        return jnp.transpose(v, (0, 2, 1, 3)).reshape(v.shape[0], -1)

    gain = columns_first(norm_gain[None])
    upstream = columns_first(lax.dynamic_slice_in_dim(cotangent, branch * share, share, 0))
    frozen, upstream = widen(columns_first(frozen), upstream, gain)

    blocks, frozen, upstream, gain = lax.optimization_barrier((blocks, frozen, upstream, gain))
    core = core.astype(jnp.int32).reshape(1)
    received = to_partner(attend(blocks, scale, 1 - core))
    attended = attend(blocks, scale, core, received)
    pieces = lax.all_to_all(
        attended.reshape(HEADS * 2, share, HEAD_DIM), CLIP + ("l",), 0, 0, tiled=True
    )
    keep, send = sum_pieces(pieces, core)
    own_part, send = project(place, keep, to_partner(send), weights)
    normed, grad = normalize(own_part, to_partner(send), frozen, upstream, gain, own)
    cot = project_back(place, grad, to_partner(grad), weights)
    parts = lax.all_gather(cot, BRANCH, axis=0, tiled=False)
    grad_attn = scatter_scaled(parts, scale)
    return normed, grad_attn[None]


def solution(mesh):
    fine = Mesh(mesh.devices.reshape(8, 2, 4, 2, 2, 2), SEQ + BRANCH)

    return jax.shard_map(
        on_device,
        mesh=fine,
        in_specs=(
            P(BRANCH, SEQ, None),
            P(BRANCH, SEQ, None),
            P(BRANCH, SEQ, None),
            P(SEQ),
            P(BRANCH),
            P(),
            P(BRANCH, SEQ),
            P(SEQ + BRANCH, None),
            P(),
            P(SEQ, None),
        ),
        out_specs=(P(SEQ + BRANCH, None), P(BRANCH, SEQ, None)),
        check_vma=False,
    )
```

```python
import math

import jax
import jax.numpy as jnp
from jax import lax
from jax.experimental import pallas as pl
from jax.experimental.pallas import tpu as pltpu
from jax.sharding import Mesh
from jax.sharding import PartitionSpec as P


HEADS = 16
HEAD_DIM = 128
EPS = 1e-06
CLIP = ("z", "y", "h")
SEQ = ("c", "z", "y", "h")
BRANCH = ("l", "k")
F32 = jnp.float32
BF16 = jnp.bfloat16
NT = (((1,), (1,)), ((), ()))


def rope_tables(positions):
    exponents = jnp.arange(HEAD_DIM // 2, dtype=F32) * (2.0 / HEAD_DIM)
    angles = positions.astype(F32)[:, None] * (10000.0 ** (-exponents))
    cosines, sines = jnp.cos(angles), jnp.sin(angles)
    return (
        jnp.concatenate([cosines, cosines], axis=1),
        jnp.concatenate([-sines, sines], axis=1),
    )


def prepare(q, k, v, cosines, sines):
    rows = q.shape[0]
    factor = math.log2(math.e) / math.sqrt(HEAD_DIM)
    group = 4

    def kernel(q_ref, k_ref, v_ref, c_ref, s_ref, o_ref):
        c, s = c_ref[...], s_ref[...]
        cq, sq = c * factor, s * factor
        for g in range(group):
            at = slice(g * HEAD_DIM, (g + 1) * HEAD_DIM)
            x = q_ref[:, at].astype(F32)
            o_ref[g, 0:rows, :] = (x * cq + pltpu.roll(x, HEAD_DIM // 2, 1) * sq).astype(BF16)
            x = k_ref[:, at].astype(F32)
            o_ref[g, rows : 2 * rows, :] = (x * c + pltpu.roll(x, HEAD_DIM // 2, 1) * s).astype(BF16)
            o_ref[g, 2 * rows :, :] = v_ref[:, at]

    column = pl.BlockSpec((rows, group * HEAD_DIM), lambda i: (0, i))
    whole = pl.BlockSpec((rows, HEAD_DIM), lambda i: (0, 0))
    return pl.pallas_call(
        kernel,
        out_shape=jax.ShapeDtypeStruct((HEADS, 3 * rows, HEAD_DIM), BF16),
        grid=(HEADS // group,),
        in_specs=[column, column, column, whole, whole],
        out_specs=pl.BlockSpec((group, 3 * rows, HEAD_DIM), lambda i: (i, 0, 0)),
        compiler_params=pltpu.CompilerParams(vmem_limit_bytes=10 << 20),
        name="prepare",
    )(q, k, v, cosines, sines)


def attend(blocks, scale, part, received=None):
    sources, three_rows, _ = blocks.shape
    rows = three_rows // 3
    length = sources * rows
    share = rows // 4
    queries = length // 2
    bq, kc, kt = 384, 512, 256
    steps = queries // bq

    def kernel(part_ref, scale_ref, b_ref, *refs):
        refs = list(refs)
        r_ref = refs.pop(0) if received is not None else None
        o_ref, q_ref, k_ref, v_ref, s_ref, m_ref = refs
        for j in range(sources):
            at = slice(j * rows, (j + 1) * rows)
            for l in range(2):
                first = pl.multiple_of((2 * l + part_ref[0]) * share, share)
                to = (2 * j + l) * share
                q_ref[to : to + share, :] = b_ref[j, pl.ds(first, share), :]
            k_ref[at, :] = b_ref[j, rows : 2 * rows, :]
            v_ref[at, 0:HEAD_DIM] = b_ref[j, 2 * rows :, :]
        v_ref[:, HEAD_DIM:] = jnp.ones((length, HEAD_DIM), BF16)

        def scores(i, slot):
            q = q_ref[pl.ds(pl.multiple_of(i * bq, bq), bq), :]
            top = None
            for j in range(length // kt):
                s = lax.dot_general(
                    q, k_ref[j * kt : (j + 1) * kt, :], NT, preferred_element_type=F32
                )
                s_ref[slot, :, j * kt : (j + 1) * kt] = s
                for half in range(kt // 128):
                    piece = s[:, half * 128 : (half + 1) * 128]
                    top = piece if top is None else jnp.maximum(top, piece)
            m_ref[slot] = jnp.broadcast_to(jnp.max(top, axis=1, keepdims=True), (bq, 128))

        def mix(i, slot):
            top = jnp.concatenate([m_ref[slot]] * (kc // 128), axis=1)
            total = None
            for j in range(length // kc):
                p = jnp.exp2(s_ref[slot, :, j * kc : (j + 1) * kc] - top).astype(BF16)
                piece = jnp.dot(p, v_ref[j * kc : (j + 1) * kc, :], preferred_element_type=F32)
                total = piece if total is None else total + piece
            out = total[:, :HEAD_DIM] * (scale_ref[0] / total[:, HEAD_DIM:])
            at = pl.ds(pl.multiple_of(i * bq, bq), bq)
            if r_ref is not None:
                out = out + r_ref[at, :].astype(F32)
            o_ref[at, :] = out.astype(BF16)

        scores(0, 0)

        def pair(t, carry):
            i = 2 * t
            scores(i + 1, 1)
            mix(i, 0)
            scores(i + 2, 0)
            mix(i + 1, 1)
            return carry

        lax.fori_loop(0, (steps - 2) // 2, pair, 0)
        scores(steps - 1, 1)
        mix(steps - 2, 0)
        mix(steps - 1, 1)

    extra = () if received is None else (received,)
    return pl.pallas_call(
        kernel,
        out_shape=jax.ShapeDtypeStruct((queries, HEAD_DIM), BF16),
        in_specs=[pl.BlockSpec(memory_space=pltpu.SMEM)] * 2
        + [pl.BlockSpec(memory_space=pltpu.VMEM)] * (1 + len(extra)),
        out_specs=pl.BlockSpec(memory_space=pltpu.VMEM),
        scratch_shapes=[
            pltpu.VMEM((queries, HEAD_DIM), BF16),
            pltpu.VMEM((length, HEAD_DIM), BF16),
            pltpu.VMEM((length, 2 * HEAD_DIM), BF16),
            pltpu.VMEM((2, bq, length), F32),
            pltpu.VMEM((2, bq, 128), F32),
        ],
        compiler_params=pltpu.CompilerParams(vmem_limit_bytes=20 << 20),
        cost_estimate=pl.CostEstimate(
            flops=4 * queries * length * HEAD_DIM,
            bytes_accessed=2 * blocks.size,
            transcendentals=queries * length,
        ),
        name="attend_last" if extra else "attend_first",
    )(part, scale, blocks, *extra)


def exchange(x, partner):
    count = math.prod(lax.axis_size(name) for name in SEQ + BRANCH)
    return lax.ppermute(x, SEQ + BRANCH, [(i, partner(i)) for i in range(count)])


def sum_pieces(pieces, core):
    _, share, _ = pieces.shape

    def kernel(core_ref, p_ref, keep_ref, send_ref):
        for out, part in ((keep_ref, core_ref[0]), (send_ref, 1 - core_ref[0])):
            for block in range(2):
                for r in range(4):
                    head = (2 * block + part) * 4 + r
                    total = p_ref[2 * head].astype(F32) + p_ref[2 * head + 1].astype(F32)
                    at = (block * 4 + r) * HEAD_DIM
                    out[:, at : at + HEAD_DIM] = total.astype(BF16)

    shape = jax.ShapeDtypeStruct((share, HEADS // 2 * HEAD_DIM), BF16)
    return pl.pallas_call(
        kernel,
        out_shape=(shape, shape),
        in_specs=[
            pl.BlockSpec(memory_space=pltpu.SMEM),
            pl.BlockSpec(memory_space=pltpu.VMEM),
        ],
        out_specs=(pl.BlockSpec(memory_space=pltpu.VMEM),) * 2,
        compiler_params=pltpu.CompilerParams(vmem_limit_bytes=4 << 20),
        name="sum_pieces",
    )(core, pieces)


def weight_block(place_ref, outer, inner):
    core, x, y = place_ref[0], place_ref[1], place_ref[2]
    first = core == 0
    x_there = x ^ jnp.where(first, outer, inner)
    y_there = y ^ jnp.where(first, inner, outer)
    return x_there % 2, y_there * 2 + x_there // 2


def project(place, keep, received, weights):
    share, rows = keep.shape
    _, columns, features = weights[0].shape

    def kernel(place_ref, keep_ref, received_ref, w0, w1, w2, w3, own_ref, send_ref, m_ref, a_ref):
        m_ref[0:share, :] = keep_ref[...]
        m_ref[share:, :] = received_ref[...]
        a_ref[...] = jnp.zeros_like(a_ref)
        for outer, w_ref in enumerate((w0, w1, w2, w3)):
            for inner in range(4):
                row, column = weight_block(place_ref, outer, inner)
                m = m_ref[:, pl.ds(pl.multiple_of(row * features, features), features)]
                at = pl.ds(pl.multiple_of(column * columns, columns), columns)
                a_ref[:, at] += lax.dot_general(
                    m, w_ref[inner], NT, preferred_element_type=F32
                )
        own_ref[...] = a_ref[0:share, :]
        send_ref[...] = a_ref[share:, :].astype(BF16)

    return pl.pallas_call(
        kernel,
        out_shape=(
            jax.ShapeDtypeStruct((share, 8 * columns), F32),
            jax.ShapeDtypeStruct((share, 8 * columns), BF16),
        ),
        in_specs=[pl.BlockSpec(memory_space=pltpu.SMEM)]
        + [pl.BlockSpec(memory_space=pltpu.VMEM)] * 6,
        out_specs=(pl.BlockSpec(memory_space=pltpu.VMEM),) * 2,
        scratch_shapes=[
            pltpu.VMEM((2 * share, rows), BF16),
            pltpu.VMEM((2 * share, 8 * columns), F32),
        ],
        compiler_params=pltpu.CompilerParams(vmem_limit_bytes=16 << 20),
        name="project",
    )(place, keep, received, *weights)


def widen(frozen, upstream, gain):
    def kernel(frozen_ref, upstream_ref, gain_ref, f_ref, u_ref):
        f_ref[...] = frozen_ref[...].astype(F32)
        u_ref[...] = upstream_ref[...].astype(F32) * gain_ref[...]

    shape = jax.ShapeDtypeStruct(frozen.shape, F32)
    return pl.pallas_call(
        kernel,
        out_shape=(shape, shape),
        in_specs=[pl.BlockSpec(memory_space=pltpu.VMEM)] * 3,
        out_specs=(pl.BlockSpec(memory_space=pltpu.VMEM),) * 2,
        compiler_params=pltpu.CompilerParams(vmem_limit_bytes=6 << 20),
        name="widen",
    )(frozen, upstream, gain)


def normalize(own, received, frozen, upstream, gain, block):
    share, width = own.shape

    def kernel(own_ref, received_ref, frozen_ref, up_ref, gain_ref, normed_ref, grad_ref, n_ref):
        hidden = own_ref[...] + received_ref[...].astype(F32) + frozen_ref[...]
        up = up_ref[...]
        inverse = lax.rsqrt(jnp.mean(hidden * hidden, axis=-1, keepdims=True) + EPS)
        inner = jnp.mean(up * hidden, axis=-1, keepdims=True)
        grad_ref[...] = (
            inverse * up - hidden * (inverse * inverse * inverse) * inner
        ).astype(BF16)
        normed = hidden * inverse * gain_ref[...]
        for z in range(16):
            for group in range(8):
                to, at = (z * 8 + group) * block, (group * 16 + z) * block
                n_ref[:, to : to + block] = normed[:, at : at + block]
        normed_ref[...] = n_ref[...].astype(BF16)

    shape = jax.ShapeDtypeStruct((share, width), BF16)
    return pl.pallas_call(
        kernel,
        out_shape=(shape, shape),
        in_specs=[pl.BlockSpec(memory_space=pltpu.VMEM)] * 5,
        out_specs=(pl.BlockSpec(memory_space=pltpu.VMEM),) * 2,
        scratch_shapes=[pltpu.VMEM((share, width), F32)],
        compiler_params=pltpu.CompilerParams(vmem_limit_bytes=8 << 20),
        name="normalize",
    )(own, received, frozen, upstream, gain)


def project_back(place, grad, received, weights):
    share, width = grad.shape
    _, columns, features = weights[0].shape

    def kernel(place_ref, grad_ref, received_ref, w0, w1, w2, w3, o_ref, g_ref, a_ref):
        core = place_ref[0]
        g_ref[pl.ds(pl.multiple_of(core * share, share), share), :] = grad_ref[...]
        g_ref[pl.ds(pl.multiple_of((1 - core) * share, share), share), :] = received_ref[...]
        a_ref[...] = jnp.zeros_like(a_ref)
        for outer, w_ref in enumerate((w0, w1, w2, w3)):
            for inner in range(4):
                row, column = weight_block(place_ref, outer, inner)
                g = g_ref[:, pl.ds(pl.multiple_of(column * columns, columns), columns)]
                a_ref[row] += jnp.dot(g, w_ref[inner], preferred_element_type=F32)
        for row in range(2):
            o_ref[:, row * features : (row + 1) * features] = a_ref[row].astype(BF16)

    return pl.pallas_call(
        kernel,
        out_shape=jax.ShapeDtypeStruct((2 * share, 2 * features), BF16),
        in_specs=[pl.BlockSpec(memory_space=pltpu.SMEM)]
        + [pl.BlockSpec(memory_space=pltpu.VMEM)] * 6,
        out_specs=pl.BlockSpec(memory_space=pltpu.VMEM),
        scratch_shapes=[
            pltpu.VMEM((2 * share, width), BF16),
            pltpu.VMEM((2, 2 * share, features), F32),
        ],
        compiler_params=pltpu.CompilerParams(vmem_limit_bytes=16 << 20),
        name="project_back",
    )(place, grad, received, *weights)


def scatter_scaled(parts, scale):
    _, tokens, rows = parts.shape
    features = rows // 2

    def kernel(scale_ref, p_ref, o_ref):
        for k in range(2):
            for row in range(2):
                at = (2 * row + k) * features
                part = p_ref[k, :, row * features : (row + 1) * features]
                o_ref[:, at : at + features] = (scale_ref[0] * part.astype(F32)).astype(BF16)

    return pl.pallas_call(
        kernel,
        out_shape=jax.ShapeDtypeStruct((2 * tokens, 2 * rows), BF16),
        grid=(2,),
        in_specs=[
            pl.BlockSpec(memory_space=pltpu.SMEM),
            pl.BlockSpec((2, tokens, rows), lambda l: (l, 0, 0)),
        ],
        out_specs=pl.BlockSpec((tokens, 2 * rows), lambda l: (l, 0)),
        compiler_params=pltpu.CompilerParams(vmem_limit_bytes=6 << 20),
        name="scatter_scaled",
    )(scale, parts)


def on_device(
    q_ctl, k_ctl, v_ctl, positions, branch_ids, cond_scale, out_weight, frozen, norm_gain, cotangent
):
    branch, core = lax.axis_index(BRANCH), lax.axis_index("k")
    y, x = lax.axis_index("y"), lax.axis_index(("h", "l"))
    share, _ = frozen.shape
    features, own = out_weight.shape
    place = jnp.stack([core, x, y]).astype(jnp.int32)
    scale = jnp.sum(
        jnp.where(jnp.arange(cond_scale.shape[0]) == branch_ids[0], cond_scale, 0.0)
    ).reshape(1)

    def to_partner(v):
        return exchange(v, lambda i: i ^ 1)

    w = jnp.broadcast_to(out_weight.T[None], (16, own, features))
    w = lax.all_to_all(w, ("c", "z"), 0, 0, tiled=True).reshape(16 * own, features)
    cosines, sines = rope_tables(positions)
    blocks = prepare(q_ctl[0], k_ctl[0], v_ctl[0], cosines, sines)
    w, blocks = lax.optimization_barrier((w, blocks))
    blocks = lax.all_to_all(blocks, CLIP, 0, 0, tiled=True)
    arrived = [exchange(w, lambda i: i ^ (r << (3 if i % 2 == 0 else 1))) for r in range(1, 4)]
    w = jnp.stack([w] + arrived)
    weights = [w] + [
        exchange(w, lambda i: i ^ (r << (1 if i % 2 == 0 else 3))) for r in range(1, 4)
    ]

    def columns_first(v):
        v = v.reshape(v.shape[0], 16, 8, own)
        return jnp.transpose(v, (0, 2, 1, 3)).reshape(v.shape[0], -1)

    gain = columns_first(norm_gain[None])
    upstream = columns_first(lax.dynamic_slice_in_dim(cotangent, branch * share, share, 0))
    frozen, upstream = widen(columns_first(frozen), upstream, gain)

    blocks, frozen, upstream, gain = lax.optimization_barrier((blocks, frozen, upstream, gain))
    core = core.astype(jnp.int32).reshape(1)
    received = to_partner(attend(blocks, scale, 1 - core))
    attended = attend(blocks, scale, core, received)
    pieces = lax.all_to_all(
        attended.reshape(HEADS * 2, share, HEAD_DIM), CLIP + ("l",), 0, 0, tiled=True
    )
    keep, send = sum_pieces(pieces, core)
    own_part, send = project(place, keep, to_partner(send), weights)
    normed, grad = normalize(own_part, to_partner(send), frozen, upstream, gain, own)
    cot = project_back(place, grad, to_partner(grad), weights)
    parts = lax.all_gather(cot, BRANCH, axis=0, tiled=False)
    grad_attn = scatter_scaled(parts, scale)
    return normed, grad_attn[None]


def solution(mesh):
    fine = Mesh(mesh.devices.reshape(8, 2, 4, 2, 2, 2), SEQ + BRANCH)

    return jax.shard_map(
        on_device,
        mesh=fine,
        in_specs=(
            P(BRANCH, SEQ, None),
            P(BRANCH, SEQ, None),
            P(BRANCH, SEQ, None),
            P(SEQ),
            P(BRANCH),
            P(),
            P(BRANCH, SEQ),
            P(SEQ + BRANCH, None),
            P(),
            P(SEQ, None),
        ),
        out_specs=(P(SEQ + BRANCH, None), P(BRANCH, SEQ, None)),
        check_vma=False,
    )
```

```python
import math

import jax
import jax.numpy as jnp
from jax import lax
from jax.experimental import pallas as pl
from jax.experimental.pallas import tpu as pltpu
from jax.sharding import Mesh
from jax.sharding import PartitionSpec as P


HEADS = 16
HEAD_DIM = 128
EPS = 1e-06
CLIP = ("z", "y", "h")
SEQ = ("c", "z", "y", "h")
BRANCH = ("l", "k")
F32 = jnp.float32
BF16 = jnp.bfloat16
NT = (((1,), (1,)), ((), ()))


def rope_tables(positions):
    exponents = jnp.arange(HEAD_DIM // 2, dtype=F32) * (2.0 / HEAD_DIM)
    angles = positions.astype(F32)[:, None] * (10000.0 ** (-exponents))
    cosines, sines = jnp.cos(angles), jnp.sin(angles)
    return (
        jnp.concatenate([cosines, cosines], axis=1),
        jnp.concatenate([-sines, sines], axis=1),
    )


def prepare(q, k, v, cosines, sines):
    rows = q.shape[0]
    factor = math.log2(math.e) / math.sqrt(HEAD_DIM)
    group = 4

    def kernel(q_ref, k_ref, v_ref, c_ref, s_ref, o_ref):
        c, s = c_ref[...], s_ref[...]
        cq, sq = c * factor, s * factor
        for g in range(group):
            at = slice(g * HEAD_DIM, (g + 1) * HEAD_DIM)
            x = q_ref[:, at].astype(F32)
            o_ref[g, 0:rows, :] = (x * cq + pltpu.roll(x, HEAD_DIM // 2, 1) * sq).astype(BF16)
            x = k_ref[:, at].astype(F32)
            o_ref[g, rows : 2 * rows, :] = (x * c + pltpu.roll(x, HEAD_DIM // 2, 1) * s).astype(BF16)
            o_ref[g, 2 * rows :, :] = v_ref[:, at]

    column = pl.BlockSpec((rows, group * HEAD_DIM), lambda i: (0, i))
    whole = pl.BlockSpec((rows, HEAD_DIM), lambda i: (0, 0))
    return pl.pallas_call(
        kernel,
        out_shape=jax.ShapeDtypeStruct((HEADS, 3 * rows, HEAD_DIM), BF16),
        grid=(HEADS // group,),
        in_specs=[column, column, column, whole, whole],
        out_specs=pl.BlockSpec((group, 3 * rows, HEAD_DIM), lambda i: (i, 0, 0)),
        compiler_params=pltpu.CompilerParams(vmem_limit_bytes=10 << 20),
        name="prepare",
    )(q, k, v, cosines, sines)


def attend(blocks, scale, part, received=None):
    sources, three_rows, _ = blocks.shape
    rows = three_rows // 3
    length = sources * rows
    share = rows // 4
    queries = length // 2
    bq, kc, kt = 384, 512, 256
    steps = queries // bq

    def kernel(part_ref, scale_ref, b_ref, *refs):
        refs = list(refs)
        r_ref = refs.pop(0) if received is not None else None
        o_ref, q_ref, k_ref, v_ref, s_ref, m_ref = refs
        for j in range(sources):
            at = slice(j * rows, (j + 1) * rows)
            for l in range(2):
                first = pl.multiple_of((2 * l + part_ref[0]) * share, share)
                to = (2 * j + l) * share
                q_ref[to : to + share, :] = b_ref[j, pl.ds(first, share), :]
            k_ref[at, :] = b_ref[j, rows : 2 * rows, :]
            v_ref[at, 0:HEAD_DIM] = b_ref[j, 2 * rows :, :]
        v_ref[:, HEAD_DIM:] = jnp.ones((length, HEAD_DIM), BF16)

        def scores(i, slot):
            q = q_ref[pl.ds(pl.multiple_of(i * bq, bq), bq), :]
            top = None
            for j in range(length // kt):
                s = lax.dot_general(
                    q, k_ref[j * kt : (j + 1) * kt, :], NT, preferred_element_type=F32
                )
                s_ref[slot, :, j * kt : (j + 1) * kt] = s
                for half in range(kt // 128):
                    piece = s[:, half * 128 : (half + 1) * 128]
                    top = piece if top is None else jnp.maximum(top, piece)
            m_ref[slot] = jnp.broadcast_to(jnp.max(top, axis=1, keepdims=True), (bq, 128))

        def mix(i, slot):
            top = jnp.concatenate([m_ref[slot]] * (kc // 128), axis=1)
            total = None
            for j in range(length // kc):
                p = jnp.exp2(s_ref[slot, :, j * kc : (j + 1) * kc] - top).astype(BF16)
                piece = jnp.dot(p, v_ref[j * kc : (j + 1) * kc, :], preferred_element_type=F32)
                total = piece if total is None else total + piece
            out = total[:, :HEAD_DIM] * (scale_ref[0] / total[:, HEAD_DIM:])
            at = pl.ds(pl.multiple_of(i * bq, bq), bq)
            if r_ref is not None:
                out = out + r_ref[at, :].astype(F32)
            o_ref[at, :] = out.astype(BF16)

        scores(0, 0)

        def pair(t, carry):
            i = 2 * t
            scores(i + 1, 1)
            mix(i, 0)
            scores(i + 2, 0)
            mix(i + 1, 1)
            return carry

        lax.fori_loop(0, (steps - 2) // 2, pair, 0)
        scores(steps - 1, 1)
        mix(steps - 2, 0)
        mix(steps - 1, 1)

    extra = () if received is None else (received,)
    return pl.pallas_call(
        kernel,
        out_shape=jax.ShapeDtypeStruct((queries, HEAD_DIM), BF16),
        in_specs=[pl.BlockSpec(memory_space=pltpu.SMEM)] * 2
        + [pl.BlockSpec(memory_space=pltpu.VMEM)] * (1 + len(extra)),
        out_specs=pl.BlockSpec(memory_space=pltpu.VMEM),
        scratch_shapes=[
            pltpu.VMEM((queries, HEAD_DIM), BF16),
            pltpu.VMEM((length, HEAD_DIM), BF16),
            pltpu.VMEM((length, 2 * HEAD_DIM), BF16),
            pltpu.VMEM((2, bq, length), F32),
            pltpu.VMEM((2, bq, 128), F32),
        ],
        compiler_params=pltpu.CompilerParams(vmem_limit_bytes=20 << 20),
        cost_estimate=pl.CostEstimate(
            flops=4 * queries * length * HEAD_DIM,
            bytes_accessed=2 * blocks.size,
            transcendentals=queries * length,
        ),
        name="attend_last" if extra else "attend_first",
    )(part, scale, blocks, *extra)


def exchange(x, partner):
    count = math.prod(lax.axis_size(name) for name in SEQ + BRANCH)
    return lax.ppermute(x, SEQ + BRANCH, [(i, partner(i)) for i in range(count)])


def sum_pieces(pieces, core):
    _, share, _ = pieces.shape

    def kernel(core_ref, p_ref, keep_ref, send_ref):
        for out, part in ((keep_ref, core_ref[0]), (send_ref, 1 - core_ref[0])):
            for block in range(2):
                for r in range(4):
                    head = (2 * block + part) * 4 + r
                    total = p_ref[2 * head].astype(F32) + p_ref[2 * head + 1].astype(F32)
                    at = (block * 4 + r) * HEAD_DIM
                    out[:, at : at + HEAD_DIM] = total.astype(BF16)

    shape = jax.ShapeDtypeStruct((share, HEADS // 2 * HEAD_DIM), BF16)
    return pl.pallas_call(
        kernel,
        out_shape=(shape, shape),
        in_specs=[
            pl.BlockSpec(memory_space=pltpu.SMEM),
            pl.BlockSpec(memory_space=pltpu.VMEM),
        ],
        out_specs=(pl.BlockSpec(memory_space=pltpu.VMEM),) * 2,
        compiler_params=pltpu.CompilerParams(vmem_limit_bytes=4 << 20),
        name="sum_pieces",
    )(core, pieces)


def weight_block(place_ref, offset, inner):
    core, x, y = place_ref[0], place_ref[1], place_ref[2]
    first = core == 0
    x_there = jnp.where(first, (x + offset) & 3, x ^ inner)
    y_there = jnp.where(first, y ^ inner, (y + offset) & 3)
    return x_there & 1, y_there * 2 + (x_there >> 1)


BUFFERS = ((0, 0, 4), (1, 0, 4), (3, 0, 4), (2, 0, 2), (2, 2, 2))


def project(place, keep, received, weights):
    share, rows = keep.shape
    _, columns, features = weights[0].shape

    def kernel(place_ref, keep_ref, received_ref, w0, w1, w2, w3, w4, own_ref, send_ref, m_ref, a_ref):
        m_ref[0:share, :] = keep_ref[...]
        m_ref[share:, :] = received_ref[...]
        a_ref[...] = jnp.zeros_like(a_ref)
        for w_ref, (offset, begin, count) in zip((w0, w1, w2, w3, w4), BUFFERS):
            for inner in range(count):
                row, column = weight_block(place_ref, offset, begin + inner)
                m = m_ref[:, pl.ds(pl.multiple_of(row * features, features), features)]
                at = pl.ds(pl.multiple_of(column * columns, columns), columns)
                a_ref[:, at] += lax.dot_general(
                    m, w_ref[inner], NT, preferred_element_type=F32
                )
        own_ref[...] = a_ref[0:share, :]
        send_ref[...] = a_ref[share:, :].astype(BF16)

    return pl.pallas_call(
        kernel,
        out_shape=(
            jax.ShapeDtypeStruct((share, 8 * columns), F32),
            jax.ShapeDtypeStruct((share, 8 * columns), BF16),
        ),
        in_specs=[pl.BlockSpec(memory_space=pltpu.SMEM)]
        + [pl.BlockSpec(memory_space=pltpu.VMEM)] * 7,
        out_specs=(pl.BlockSpec(memory_space=pltpu.VMEM),) * 2,
        scratch_shapes=[
            pltpu.VMEM((2 * share, rows), BF16),
            pltpu.VMEM((2 * share, 8 * columns), F32),
        ],
        compiler_params=pltpu.CompilerParams(vmem_limit_bytes=16 << 20),
        name="project",
    )(place, keep, received, *weights)


def widen(frozen, upstream, gain):
    def kernel(frozen_ref, upstream_ref, gain_ref, f_ref, u_ref):
        f_ref[...] = frozen_ref[...].astype(F32)
        u_ref[...] = upstream_ref[...].astype(F32) * gain_ref[...]

    shape = jax.ShapeDtypeStruct(frozen.shape, F32)
    return pl.pallas_call(
        kernel,
        out_shape=(shape, shape),
        in_specs=[pl.BlockSpec(memory_space=pltpu.VMEM)] * 3,
        out_specs=(pl.BlockSpec(memory_space=pltpu.VMEM),) * 2,
        compiler_params=pltpu.CompilerParams(vmem_limit_bytes=6 << 20),
        name="widen",
    )(frozen, upstream, gain)


def normalize(own, received, frozen, upstream, gain, block):
    share, width = own.shape

    def kernel(own_ref, received_ref, frozen_ref, up_ref, gain_ref, normed_ref, grad_ref, n_ref):
        hidden = own_ref[...] + received_ref[...].astype(F32) + frozen_ref[...]
        up = up_ref[...]
        inverse = lax.rsqrt(jnp.mean(hidden * hidden, axis=-1, keepdims=True) + EPS)
        inner = jnp.mean(up * hidden, axis=-1, keepdims=True)
        grad_ref[...] = (
            inverse * up - hidden * (inverse * inverse * inverse) * inner
        ).astype(BF16)
        normed = hidden * inverse * gain_ref[...]
        for z in range(16):
            for group in range(8):
                to, at = (z * 8 + group) * block, (group * 16 + z) * block
                n_ref[:, to : to + block] = normed[:, at : at + block]
        normed_ref[...] = n_ref[...].astype(BF16)

    shape = jax.ShapeDtypeStruct((share, width), BF16)
    return pl.pallas_call(
        kernel,
        out_shape=(shape, shape),
        in_specs=[pl.BlockSpec(memory_space=pltpu.VMEM)] * 5,
        out_specs=(pl.BlockSpec(memory_space=pltpu.VMEM),) * 2,
        scratch_shapes=[pltpu.VMEM((share, width), F32)],
        compiler_params=pltpu.CompilerParams(vmem_limit_bytes=8 << 20),
        name="normalize",
    )(own, received, frozen, upstream, gain)


def project_back(place, grad, received, weights):
    share, width = grad.shape
    _, columns, features = weights[0].shape

    def kernel(place_ref, grad_ref, received_ref, w0, w1, w2, w3, w4, o_ref, g_ref, a_ref):
        core = place_ref[0]
        g_ref[pl.ds(pl.multiple_of(core * share, share), share), :] = grad_ref[...]
        g_ref[pl.ds(pl.multiple_of((1 - core) * share, share), share), :] = received_ref[...]
        a_ref[...] = jnp.zeros_like(a_ref)
        for w_ref, (offset, begin, count) in zip((w0, w1, w2, w3, w4), BUFFERS):
            for inner in range(count):
                row, column = weight_block(place_ref, offset, begin + inner)
                g = g_ref[:, pl.ds(pl.multiple_of(column * columns, columns), columns)]
                a_ref[row] += jnp.dot(g, w_ref[inner], preferred_element_type=F32)
        for row in range(2):
            o_ref[:, row * features : (row + 1) * features] = a_ref[row].astype(BF16)

    return pl.pallas_call(
        kernel,
        out_shape=jax.ShapeDtypeStruct((2 * share, 2 * features), BF16),
        in_specs=[pl.BlockSpec(memory_space=pltpu.SMEM)]
        + [pl.BlockSpec(memory_space=pltpu.VMEM)] * 7,
        out_specs=pl.BlockSpec(memory_space=pltpu.VMEM),
        scratch_shapes=[
            pltpu.VMEM((2 * share, width), BF16),
            pltpu.VMEM((2, 2 * share, features), F32),
        ],
        compiler_params=pltpu.CompilerParams(vmem_limit_bytes=16 << 20),
        name="project_back",
    )(place, grad, received, *weights)


def scatter_scaled(parts, scale):
    _, tokens, rows = parts.shape
    features = rows // 2

    def kernel(scale_ref, p_ref, o_ref):
        for k in range(2):
            for row in range(2):
                at = (2 * row + k) * features
                part = p_ref[k, :, row * features : (row + 1) * features]
                o_ref[:, at : at + features] = (scale_ref[0] * part.astype(F32)).astype(BF16)

    return pl.pallas_call(
        kernel,
        out_shape=jax.ShapeDtypeStruct((2 * tokens, 2 * rows), BF16),
        grid=(2,),
        in_specs=[
            pl.BlockSpec(memory_space=pltpu.SMEM),
            pl.BlockSpec((2, tokens, rows), lambda l: (l, 0, 0)),
        ],
        out_specs=pl.BlockSpec((tokens, 2 * rows), lambda l: (l, 0)),
        compiler_params=pltpu.CompilerParams(vmem_limit_bytes=6 << 20),
        name="scatter_scaled",
    )(scale, parts)


def on_device(
    q_ctl, k_ctl, v_ctl, positions, branch_ids, cond_scale, out_weight, frozen, norm_gain, cotangent
):
    branch, core = lax.axis_index(BRANCH), lax.axis_index("k")
    y, x = lax.axis_index("y"), lax.axis_index(("h", "l"))
    share, _ = frozen.shape
    features, own = out_weight.shape
    place = jnp.stack([core, x, y]).astype(jnp.int32)
    scale = jnp.sum(
        jnp.where(jnp.arange(cond_scale.shape[0]) == branch_ids[0], cond_scale, 0.0)
    ).reshape(1)

    def to_partner(v):
        return exchange(v, lambda i: i ^ 1)

    w = jnp.broadcast_to(out_weight.T[None], (16, own, features))
    w = lax.all_to_all(w, ("c", "z"), 0, 0, tiled=True).reshape(16 * own, features)
    cosines, sines = rope_tables(positions)
    blocks = prepare(q_ctl[0], k_ctl[0], v_ctl[0], cosines, sines)
    w, blocks = lax.optimization_barrier((w, blocks))
    blocks = lax.all_to_all(blocks, CLIP, 0, 0, tiled=True)
    arrived = [exchange(w, lambda i: i ^ (r << (3 if i % 2 == 0 else 1))) for r in range(1, 4)]
    w = jnp.stack([w] + arrived)

    def along(step):
        def partner(i):
            low = 3 if i % 2 else 1
            return i + ((((i >> low) + step) & 3) - ((i >> low) & 3) << low)

        return partner

    up, down = exchange(w, along(-1)), exchange(w, along(1))
    weights = [w, up, down, exchange(up[:2], along(-1)), exchange(down[2:], along(1))]

    def columns_first(v):
        v = v.reshape(v.shape[0], 16, 8, own)
        return jnp.transpose(v, (0, 2, 1, 3)).reshape(v.shape[0], -1)

    gain = columns_first(norm_gain[None])
    upstream = columns_first(lax.dynamic_slice_in_dim(cotangent, branch * share, share, 0))
    frozen, upstream = widen(columns_first(frozen), upstream, gain)

    blocks, frozen, upstream, gain = lax.optimization_barrier((blocks, frozen, upstream, gain))
    core = core.astype(jnp.int32).reshape(1)
    received = to_partner(attend(blocks, scale, 1 - core))
    attended = attend(blocks, scale, core, received)
    pieces = lax.all_to_all(
        attended.reshape(HEADS * 2, share, HEAD_DIM), CLIP + ("l",), 0, 0, tiled=True
    )
    keep, send = sum_pieces(pieces, core)
    own_part, send = project(place, keep, to_partner(send), weights)
    normed, grad = normalize(own_part, to_partner(send), frozen, upstream, gain, own)
    cot = project_back(place, grad, to_partner(grad), weights)
    parts = lax.all_gather(cot, BRANCH, axis=0, tiled=False)
    grad_attn = scatter_scaled(parts, scale)
    return normed, grad_attn[None]


def solution(mesh):
    fine = Mesh(mesh.devices.reshape(8, 2, 4, 2, 2, 2), SEQ + BRANCH)

    return jax.shard_map(
        on_device,
        mesh=fine,
        in_specs=(
            P(BRANCH, SEQ, None),
            P(BRANCH, SEQ, None),
            P(BRANCH, SEQ, None),
            P(SEQ),
            P(BRANCH),
            P(),
            P(BRANCH, SEQ),
            P(SEQ + BRANCH, None),
            P(),
            P(SEQ, None),
        ),
        out_specs=(P(SEQ + BRANCH, None), P(BRANCH, SEQ, None)),
        check_vma=False,
    )
```

```python
import math

import jax
import jax.numpy as jnp
from jax import lax
from jax.experimental import pallas as pl
from jax.experimental.pallas import tpu as pltpu
from jax.sharding import Mesh
from jax.sharding import PartitionSpec as P


HEADS = 16
HEAD_DIM = 128
EPS = 1e-06
CLIP = ("z", "y", "h")
SEQ = ("c", "z", "y", "h")
BRANCH = ("l", "k")
F32 = jnp.float32
BF16 = jnp.bfloat16
NT = (((1,), (1,)), ((), ()))


def rope_tables(positions):
    exponents = jnp.arange(HEAD_DIM // 2, dtype=F32) * (2.0 / HEAD_DIM)
    angles = positions.astype(F32)[:, None] * (10000.0 ** (-exponents))
    cosines, sines = jnp.cos(angles), jnp.sin(angles)
    return (
        jnp.concatenate([cosines, cosines], axis=1),
        jnp.concatenate([-sines, sines], axis=1),
    )


def prepare(q, k, v, cosines, sines):
    rows = q.shape[0]
    factor = math.log2(math.e) / math.sqrt(HEAD_DIM)
    group = 4

    def kernel(q_ref, k_ref, v_ref, c_ref, s_ref, o_ref):
        c, s = c_ref[...], s_ref[...]
        cq, sq = c * factor, s * factor
        for g in range(group):
            at = slice(g * HEAD_DIM, (g + 1) * HEAD_DIM)
            x = q_ref[:, at].astype(F32)
            o_ref[g, 0:rows, :] = (x * cq + pltpu.roll(x, HEAD_DIM // 2, 1) * sq).astype(BF16)
            x = k_ref[:, at].astype(F32)
            o_ref[g, rows : 2 * rows, :] = (x * c + pltpu.roll(x, HEAD_DIM // 2, 1) * s).astype(BF16)
            o_ref[g, 2 * rows :, :] = v_ref[:, at]

    column = pl.BlockSpec((rows, group * HEAD_DIM), lambda i: (0, i))
    whole = pl.BlockSpec((rows, HEAD_DIM), lambda i: (0, 0))
    return pl.pallas_call(
        kernel,
        out_shape=jax.ShapeDtypeStruct((HEADS, 3 * rows, HEAD_DIM), BF16),
        grid=(HEADS // group,),
        in_specs=[column, column, column, whole, whole],
        out_specs=pl.BlockSpec((group, 3 * rows, HEAD_DIM), lambda i: (i, 0, 0)),
        compiler_params=pltpu.CompilerParams(vmem_limit_bytes=10 << 20),
        name="prepare",
    )(q, k, v, cosines, sines)


def attend(blocks, scale, part, received=None):
    sources, three_rows, _ = blocks.shape
    rows = three_rows // 3
    length = sources * rows
    share = rows // 4
    queries = length // 2
    bq, kc, kt = 384, 512, 256
    steps = queries // bq

    def kernel(part_ref, scale_ref, b_ref, *refs):
        refs = list(refs)
        r_ref = refs.pop(0) if received is not None else None
        o_ref, q_ref, k_ref, v_ref, s_ref, m_ref = refs
        for j in range(sources):
            at = slice(j * rows, (j + 1) * rows)
            for l in range(2):
                first = pl.multiple_of((2 * l + part_ref[0]) * share, share)
                to = (2 * j + l) * share
                q_ref[to : to + share, :] = b_ref[j, pl.ds(first, share), :]
            k_ref[at, :] = b_ref[j, rows : 2 * rows, :]
            v_ref[at, 0:HEAD_DIM] = b_ref[j, 2 * rows :, :]
        v_ref[:, HEAD_DIM:] = jnp.ones((length, HEAD_DIM), BF16)

        def scores(i, slot):
            q = q_ref[pl.ds(pl.multiple_of(i * bq, bq), bq), :]
            top = None
            for j in range(length // kt):
                s = lax.dot_general(
                    q, k_ref[j * kt : (j + 1) * kt, :], NT, preferred_element_type=F32
                )
                s_ref[slot, :, j * kt : (j + 1) * kt] = s
                for half in range(kt // 128):
                    piece = s[:, half * 128 : (half + 1) * 128]
                    top = piece if top is None else jnp.maximum(top, piece)
            m_ref[slot] = jnp.broadcast_to(jnp.max(top, axis=1, keepdims=True), (bq, 128))

        def mix(i, slot):
            top = jnp.concatenate([m_ref[slot]] * (kc // 128), axis=1)
            total = None
            for j in range(length // kc):
                p = jnp.exp2(s_ref[slot, :, j * kc : (j + 1) * kc] - top).astype(BF16)
                piece = jnp.dot(p, v_ref[j * kc : (j + 1) * kc, :], preferred_element_type=F32)
                total = piece if total is None else total + piece
            out = total[:, :HEAD_DIM] * (scale_ref[0] / total[:, HEAD_DIM:])
            at = pl.ds(pl.multiple_of(i * bq, bq), bq)
            if r_ref is not None:
                out = out + r_ref[at, :].astype(F32)
            o_ref[at, :] = out.astype(BF16)

        scores(0, 0)

        def pair(t, carry):
            i = 2 * t
            scores(i + 1, 1)
            mix(i, 0)
            scores(i + 2, 0)
            mix(i + 1, 1)
            return carry

        lax.fori_loop(0, (steps - 2) // 2, pair, 0)
        scores(steps - 1, 1)
        mix(steps - 2, 0)
        mix(steps - 1, 1)

    extra = () if received is None else (received,)
    return pl.pallas_call(
        kernel,
        out_shape=jax.ShapeDtypeStruct((queries, HEAD_DIM), BF16),
        in_specs=[pl.BlockSpec(memory_space=pltpu.SMEM)] * 2
        + [pl.BlockSpec(memory_space=pltpu.VMEM)] * (1 + len(extra)),
        out_specs=pl.BlockSpec(memory_space=pltpu.VMEM),
        scratch_shapes=[
            pltpu.VMEM((queries, HEAD_DIM), BF16),
            pltpu.VMEM((length, HEAD_DIM), BF16),
            pltpu.VMEM((length, 2 * HEAD_DIM), BF16),
            pltpu.VMEM((2, bq, length), F32),
            pltpu.VMEM((2, bq, 128), F32),
        ],
        compiler_params=pltpu.CompilerParams(vmem_limit_bytes=20 << 20),
        cost_estimate=pl.CostEstimate(
            flops=4 * queries * length * HEAD_DIM,
            bytes_accessed=2 * blocks.size,
            transcendentals=queries * length,
        ),
        name="attend_last" if extra else "attend_first",
    )(part, scale, blocks, *extra)


def exchange(x, partner):
    count = math.prod(lax.axis_size(name) for name in SEQ + BRANCH)
    return lax.ppermute(x, SEQ + BRANCH, [(i, partner(i)) for i in range(count)])


def sum_pieces(pieces, core):
    _, share, _ = pieces.shape

    def kernel(core_ref, p_ref, keep_ref, send_ref):
        for out, part in ((keep_ref, core_ref[0]), (send_ref, 1 - core_ref[0])):
            for block in range(2):
                for r in range(4):
                    head = (2 * block + part) * 4 + r
                    total = p_ref[2 * head].astype(F32) + p_ref[2 * head + 1].astype(F32)
                    at = (block * 4 + r) * HEAD_DIM
                    out[:, at : at + HEAD_DIM] = total.astype(BF16)

    shape = jax.ShapeDtypeStruct((share, HEADS // 2 * HEAD_DIM), BF16)
    return pl.pallas_call(
        kernel,
        out_shape=(shape, shape),
        in_specs=[
            pl.BlockSpec(memory_space=pltpu.SMEM),
            pl.BlockSpec(memory_space=pltpu.VMEM),
        ],
        out_specs=(pl.BlockSpec(memory_space=pltpu.VMEM),) * 2,
        compiler_params=pltpu.CompilerParams(vmem_limit_bytes=4 << 20),
        name="sum_pieces",
    )(core, pieces)


def weight_block(place_ref, offset, inner):
    core, x, y = place_ref[0], place_ref[1], place_ref[2]
    first = core == 0
    x_there = jnp.where(first, (x + offset) & 3, x ^ inner)
    y_there = jnp.where(first, y ^ inner, (y + offset) & 3)
    return x_there & 1, y_there * 2 + (x_there >> 1)


BUFFERS = tuple((offset, begin, 2) for offset in (0, 1, 3, 2) for begin in (0, 2))


def project(place, keep, received, weights):
    share, rows = keep.shape
    _, columns, features = weights[0].shape

    def kernel(place_ref, keep_ref, received_ref, *refs):
        *w_refs, own_ref, send_ref, m_ref, a_ref = refs
        m_ref[0:share, :] = keep_ref[...]
        m_ref[share:, :] = received_ref[...]
        a_ref[...] = jnp.zeros_like(a_ref)
        for w_ref, (offset, begin, count) in zip(w_refs, BUFFERS):
            for inner in range(count):
                row, column = weight_block(place_ref, offset, begin + inner)
                m = m_ref[:, pl.ds(pl.multiple_of(row * features, features), features)]
                at = pl.ds(pl.multiple_of(column * columns, columns), columns)
                a_ref[:, at] += lax.dot_general(
                    m, w_ref[inner], NT, preferred_element_type=F32
                )
        own_ref[...] = a_ref[0:share, :]
        send_ref[...] = a_ref[share:, :].astype(BF16)

    return pl.pallas_call(
        kernel,
        out_shape=(
            jax.ShapeDtypeStruct((share, 8 * columns), F32),
            jax.ShapeDtypeStruct((share, 8 * columns), BF16),
        ),
        in_specs=[pl.BlockSpec(memory_space=pltpu.SMEM)]
        + [pl.BlockSpec(memory_space=pltpu.VMEM)] * (2 + len(weights)),
        out_specs=(pl.BlockSpec(memory_space=pltpu.VMEM),) * 2,
        scratch_shapes=[
            pltpu.VMEM((2 * share, rows), BF16),
            pltpu.VMEM((2 * share, 8 * columns), F32),
        ],
        compiler_params=pltpu.CompilerParams(vmem_limit_bytes=16 << 20),
        name="project",
    )(place, keep, received, *weights)


def widen(frozen, upstream, gain):
    def kernel(frozen_ref, upstream_ref, gain_ref, f_ref, u_ref):
        f_ref[...] = frozen_ref[...].astype(F32)
        u_ref[...] = upstream_ref[...].astype(F32) * gain_ref[...]

    shape = jax.ShapeDtypeStruct(frozen.shape, F32)
    return pl.pallas_call(
        kernel,
        out_shape=(shape, shape),
        in_specs=[pl.BlockSpec(memory_space=pltpu.VMEM)] * 3,
        out_specs=(pl.BlockSpec(memory_space=pltpu.VMEM),) * 2,
        compiler_params=pltpu.CompilerParams(vmem_limit_bytes=6 << 20),
        name="widen",
    )(frozen, upstream, gain)


def normalize(own, received, frozen, upstream, gain, block):
    share, width = own.shape

    def kernel(own_ref, received_ref, frozen_ref, up_ref, gain_ref, normed_ref, grad_ref, n_ref):
        hidden = own_ref[...] + received_ref[...].astype(F32) + frozen_ref[...]
        up = up_ref[...]
        inverse = lax.rsqrt(jnp.mean(hidden * hidden, axis=-1, keepdims=True) + EPS)
        inner = jnp.mean(up * hidden, axis=-1, keepdims=True)
        grad_ref[...] = (
            inverse * up - hidden * (inverse * inverse * inverse) * inner
        ).astype(BF16)
        normed = hidden * inverse * gain_ref[...]
        for z in range(16):
            for group in range(8):
                to, at = (z * 8 + group) * block, (group * 16 + z) * block
                n_ref[:, to : to + block] = normed[:, at : at + block]
        normed_ref[...] = n_ref[...].astype(BF16)

    shape = jax.ShapeDtypeStruct((share, width), BF16)
    return pl.pallas_call(
        kernel,
        out_shape=(shape, shape),
        in_specs=[pl.BlockSpec(memory_space=pltpu.VMEM)] * 5,
        out_specs=(pl.BlockSpec(memory_space=pltpu.VMEM),) * 2,
        scratch_shapes=[pltpu.VMEM((share, width), F32)],
        compiler_params=pltpu.CompilerParams(vmem_limit_bytes=8 << 20),
        name="normalize",
    )(own, received, frozen, upstream, gain)


def project_back(place, grad, received, weights):
    share, width = grad.shape
    _, columns, features = weights[0].shape

    def kernel(place_ref, grad_ref, received_ref, *refs):
        *w_refs, o_ref, g_ref, a_ref = refs
        core = place_ref[0]
        g_ref[pl.ds(pl.multiple_of(core * share, share), share), :] = grad_ref[...]
        g_ref[pl.ds(pl.multiple_of((1 - core) * share, share), share), :] = received_ref[...]
        a_ref[...] = jnp.zeros_like(a_ref)
        for w_ref, (offset, begin, count) in zip(w_refs, BUFFERS):
            for inner in range(count):
                row, column = weight_block(place_ref, offset, begin + inner)
                g = g_ref[:, pl.ds(pl.multiple_of(column * columns, columns), columns)]
                a_ref[row] += jnp.dot(g, w_ref[inner], preferred_element_type=F32)
        for row in range(2):
            o_ref[:, row * features : (row + 1) * features] = a_ref[row].astype(BF16)

    return pl.pallas_call(
        kernel,
        out_shape=jax.ShapeDtypeStruct((2 * share, 2 * features), BF16),
        in_specs=[pl.BlockSpec(memory_space=pltpu.SMEM)]
        + [pl.BlockSpec(memory_space=pltpu.VMEM)] * (2 + len(weights)),
        out_specs=pl.BlockSpec(memory_space=pltpu.VMEM),
        scratch_shapes=[
            pltpu.VMEM((2 * share, width), BF16),
            pltpu.VMEM((2, 2 * share, features), F32),
        ],
        compiler_params=pltpu.CompilerParams(vmem_limit_bytes=16 << 20),
        name="project_back",
    )(place, grad, received, *weights)


def scatter_scaled(parts, scale):
    _, tokens, rows = parts.shape
    features = rows // 2

    def kernel(scale_ref, p_ref, o_ref):
        for k in range(2):
            for row in range(2):
                at = (2 * row + k) * features
                part = p_ref[k, :, row * features : (row + 1) * features]
                o_ref[:, at : at + features] = (scale_ref[0] * part.astype(F32)).astype(BF16)

    return pl.pallas_call(
        kernel,
        out_shape=jax.ShapeDtypeStruct((2 * tokens, 2 * rows), BF16),
        grid=(2,),
        in_specs=[
            pl.BlockSpec(memory_space=pltpu.SMEM),
            pl.BlockSpec((2, tokens, rows), lambda l: (l, 0, 0)),
        ],
        out_specs=pl.BlockSpec((tokens, 2 * rows), lambda l: (l, 0)),
        compiler_params=pltpu.CompilerParams(vmem_limit_bytes=6 << 20),
        name="scatter_scaled",
    )(scale, parts)


def on_device(
    q_ctl, k_ctl, v_ctl, positions, branch_ids, cond_scale, out_weight, frozen, norm_gain, cotangent
):
    branch, core = lax.axis_index(BRANCH), lax.axis_index("k")
    y, x = lax.axis_index("y"), lax.axis_index(("h", "l"))
    share, _ = frozen.shape
    features, own = out_weight.shape
    place = jnp.stack([core, x, y]).astype(jnp.int32)
    scale = jnp.sum(
        jnp.where(jnp.arange(cond_scale.shape[0]) == branch_ids[0], cond_scale, 0.0)
    ).reshape(1)

    def to_partner(v):
        return exchange(v, lambda i: i ^ 1)

    w = jnp.broadcast_to(out_weight.T[None], (16, own, features))
    w = lax.all_to_all(w, ("c", "z"), 0, 0, tiled=True).reshape(16 * own, features)
    cosines, sines = rope_tables(positions)
    blocks = prepare(q_ctl[0], k_ctl[0], v_ctl[0], cosines, sines)
    w, blocks = lax.optimization_barrier((w, blocks))
    blocks = lax.all_to_all(blocks, CLIP, 0, 0, tiled=True)
    arrived = [exchange(w, lambda i: i ^ (r << (3 if i % 2 == 0 else 1))) for r in range(1, 4)]
    low, high = jnp.stack([w, arrived[0]]), jnp.stack(arrived[1:])

    def along(step):
        def partner(i):
            low = 3 if i % 2 else 1
            return i + ((((i >> low) + step) & 3) - ((i >> low) & 3) << low)

        return partner

    up_low, down_high = exchange(low, along(-1)), exchange(high, along(1))
    up_high, down_low = exchange(high, along(-1)), exchange(low, along(1))
    far_low, far_high = exchange(up_low, along(-1)), exchange(down_high, along(1))
    weights = [low, high, up_low, up_high, down_low, down_high, far_low, far_high]

    def columns_first(v):
        v = v.reshape(v.shape[0], 16, 8, own)
        return jnp.transpose(v, (0, 2, 1, 3)).reshape(v.shape[0], -1)

    gain = columns_first(norm_gain[None])
    upstream = columns_first(lax.dynamic_slice_in_dim(cotangent, branch * share, share, 0))
    frozen, upstream = widen(columns_first(frozen), upstream, gain)

    blocks, frozen, upstream, gain = lax.optimization_barrier((blocks, frozen, upstream, gain))
    core = core.astype(jnp.int32).reshape(1)
    received = to_partner(attend(blocks, scale, 1 - core))
    attended = attend(blocks, scale, core, received)
    pieces = lax.all_to_all(
        attended.reshape(HEADS * 2, share, HEAD_DIM), CLIP + ("l",), 0, 0, tiled=True
    )
    keep, send = sum_pieces(pieces, core)
    own_part, send = project(place, keep, to_partner(send), weights)
    normed, grad = normalize(own_part, to_partner(send), frozen, upstream, gain, own)
    cot = project_back(place, grad, to_partner(grad), weights)
    parts = lax.all_gather(cot, BRANCH, axis=0, tiled=False)
    grad_attn = scatter_scaled(parts, scale)
    return normed, grad_attn[None]


def solution(mesh):
    fine = Mesh(mesh.devices.reshape(8, 2, 4, 2, 2, 2), SEQ + BRANCH)

    return jax.shard_map(
        on_device,
        mesh=fine,
        in_specs=(
            P(BRANCH, SEQ, None),
            P(BRANCH, SEQ, None),
            P(BRANCH, SEQ, None),
            P(SEQ),
            P(BRANCH),
            P(),
            P(BRANCH, SEQ),
            P(SEQ + BRANCH, None),
            P(),
            P(SEQ, None),
        ),
        out_specs=(P(SEQ + BRANCH, None), P(BRANCH, SEQ, None)),
        check_vma=False,
    )
```

```python
import math

import jax
import jax.numpy as jnp
from jax import lax
from jax.experimental import pallas as pl
from jax.experimental.pallas import tpu as pltpu
from jax.sharding import Mesh
from jax.sharding import PartitionSpec as P


HEADS = 16
HEAD_DIM = 128
EPS = 1e-06
CLIP = ("z", "y", "h")
SEQ = ("c", "z", "y", "h")
BRANCH = ("l", "k")
F32 = jnp.float32
BF16 = jnp.bfloat16
NT = (((1,), (1,)), ((), ()))


def rope_tables(positions):
    exponents = jnp.arange(HEAD_DIM // 2, dtype=F32) * (2.0 / HEAD_DIM)
    angles = positions.astype(F32)[:, None] * (10000.0 ** (-exponents))
    cosines, sines = jnp.cos(angles), jnp.sin(angles)
    return (
        jnp.concatenate([cosines, cosines], axis=1),
        jnp.concatenate([-sines, sines], axis=1),
    )


def prepare(q, k, v, cosines, sines):
    rows = q.shape[0]
    factor = math.log2(math.e) / math.sqrt(HEAD_DIM)
    group = 4

    def kernel(q_ref, k_ref, v_ref, c_ref, s_ref, o_ref):
        c, s = c_ref[...], s_ref[...]
        cq, sq = c * factor, s * factor
        for g in range(group):
            at = slice(g * HEAD_DIM, (g + 1) * HEAD_DIM)
            x = q_ref[:, at].astype(F32)
            o_ref[g, 0:rows, :] = (x * cq + pltpu.roll(x, HEAD_DIM // 2, 1) * sq).astype(BF16)
            x = k_ref[:, at].astype(F32)
            o_ref[g, rows : 2 * rows, :] = (x * c + pltpu.roll(x, HEAD_DIM // 2, 1) * s).astype(BF16)
            o_ref[g, 2 * rows :, :] = v_ref[:, at]

    column = pl.BlockSpec((rows, group * HEAD_DIM), lambda i: (0, i))
    whole = pl.BlockSpec((rows, HEAD_DIM), lambda i: (0, 0))
    return pl.pallas_call(
        kernel,
        out_shape=jax.ShapeDtypeStruct((HEADS, 3 * rows, HEAD_DIM), BF16),
        grid=(HEADS // group,),
        in_specs=[column, column, column, whole, whole],
        out_specs=pl.BlockSpec((group, 3 * rows, HEAD_DIM), lambda i: (i, 0, 0)),
        compiler_params=pltpu.CompilerParams(vmem_limit_bytes=10 << 20),
        name="prepare",
    )(q, k, v, cosines, sines)


def attend(blocks, scale, part, received=None):
    sources, three_rows, _ = blocks.shape
    rows = three_rows // 3
    length = sources * rows
    share = rows // 4
    queries = length // 2
    bq, kc, kt = 384, 512, 256
    steps = queries // bq

    def kernel(part_ref, scale_ref, b_ref, *refs):
        refs = list(refs)
        r_ref = refs.pop(0) if received is not None else None
        o_ref, q_ref, k_ref, v_ref, s_ref, m_ref = refs
        for j in range(sources):
            at = slice(j * rows, (j + 1) * rows)
            for l in range(2):
                first = pl.multiple_of((2 * l + part_ref[0]) * share, share)
                to = (2 * j + l) * share
                q_ref[to : to + share, :] = b_ref[j, pl.ds(first, share), :]
            k_ref[at, :] = b_ref[j, rows : 2 * rows, :]
            v_ref[at, 0:HEAD_DIM] = b_ref[j, 2 * rows :, :]
        v_ref[:, HEAD_DIM:] = jnp.ones((length, HEAD_DIM), BF16)

        def scores(i, slot):
            q = q_ref[pl.ds(pl.multiple_of(i * bq, bq), bq), :]
            top = None
            for j in range(length // kt):
                s = lax.dot_general(
                    q, k_ref[j * kt : (j + 1) * kt, :], NT, preferred_element_type=F32
                )
                s_ref[slot, :, j * kt : (j + 1) * kt] = s
                for half in range(kt // 128):
                    piece = s[:, half * 128 : (half + 1) * 128]
                    top = piece if top is None else jnp.maximum(top, piece)
            m_ref[slot] = jnp.broadcast_to(jnp.max(top, axis=1, keepdims=True), (bq, 128))

        def mix(i, slot):
            top = jnp.concatenate([m_ref[slot]] * (kc // 128), axis=1)
            total = None
            for j in range(length // kc):
                p = jnp.exp2(s_ref[slot, :, j * kc : (j + 1) * kc] - top).astype(BF16)
                piece = jnp.dot(p, v_ref[j * kc : (j + 1) * kc, :], preferred_element_type=F32)
                total = piece if total is None else total + piece
            out = total[:, :HEAD_DIM] * (scale_ref[0] / total[:, HEAD_DIM:])
            at = pl.ds(pl.multiple_of(i * bq, bq), bq)
            if r_ref is not None:
                out = out + r_ref[at, :].astype(F32)
            o_ref[at, :] = out.astype(BF16)

        scores(0, 0)

        def pair(t, carry):
            i = 2 * t
            scores(i + 1, 1)
            mix(i, 0)
            scores(i + 2, 0)
            mix(i + 1, 1)
            return carry

        lax.fori_loop(0, (steps - 2) // 2, pair, 0)
        scores(steps - 1, 1)
        mix(steps - 2, 0)
        mix(steps - 1, 1)

    extra = () if received is None else (received,)
    return pl.pallas_call(
        kernel,
        out_shape=jax.ShapeDtypeStruct((queries, HEAD_DIM), BF16),
        in_specs=[pl.BlockSpec(memory_space=pltpu.SMEM)] * 2
        + [pl.BlockSpec(memory_space=pltpu.VMEM)] * (1 + len(extra)),
        out_specs=pl.BlockSpec(memory_space=pltpu.VMEM),
        scratch_shapes=[
            pltpu.VMEM((queries, HEAD_DIM), BF16),
            pltpu.VMEM((length, HEAD_DIM), BF16),
            pltpu.VMEM((length, 2 * HEAD_DIM), BF16),
            pltpu.VMEM((2, bq, length), F32),
            pltpu.VMEM((2, bq, 128), F32),
        ],
        compiler_params=pltpu.CompilerParams(vmem_limit_bytes=20 << 20),
        cost_estimate=pl.CostEstimate(
            flops=4 * queries * length * HEAD_DIM,
            bytes_accessed=2 * blocks.size,
            transcendentals=queries * length,
        ),
        name="attend_last" if extra else "attend_first",
    )(part, scale, blocks, *extra)


def exchange(x, partner):
    count = math.prod(lax.axis_size(name) for name in SEQ + BRANCH)
    return lax.ppermute(x, SEQ + BRANCH, [(i, partner(i)) for i in range(count)])


def sum_pieces(pieces, core):
    _, share, _ = pieces.shape

    def kernel(core_ref, p_ref, keep_ref, send_ref):
        for out, part in ((keep_ref, core_ref[0]), (send_ref, 1 - core_ref[0])):
            for block in range(2):
                for r in range(4):
                    head = (2 * block + part) * 4 + r
                    total = p_ref[2 * head].astype(F32) + p_ref[2 * head + 1].astype(F32)
                    at = (block * 4 + r) * HEAD_DIM
                    out[:, at : at + HEAD_DIM] = total.astype(BF16)

    shape = jax.ShapeDtypeStruct((share, HEADS // 2 * HEAD_DIM), BF16)
    return pl.pallas_call(
        kernel,
        out_shape=(shape, shape),
        in_specs=[
            pl.BlockSpec(memory_space=pltpu.SMEM),
            pl.BlockSpec(memory_space=pltpu.VMEM),
        ],
        out_specs=(pl.BlockSpec(memory_space=pltpu.VMEM),) * 2,
        compiler_params=pltpu.CompilerParams(vmem_limit_bytes=4 << 20),
        name="sum_pieces",
    )(core, pieces)


def weight_block(place_ref, offset, inner):
    core, x, y = place_ref[0], place_ref[1], place_ref[2]
    first = core == 0
    x_there = jnp.where(first, (x + offset) & 3, x ^ inner)
    y_there = jnp.where(first, y ^ inner, (y + offset) & 3)
    return x_there & 1, y_there * 2 + (x_there >> 1)


BUFFERS = ((0, 0, 4), (1, 0, 4), (3, 0, 4), (2, 0, 4))


def project(place, keep, received, weights):
    share, rows = keep.shape
    _, columns, features = weights[0].shape

    def kernel(place_ref, keep_ref, received_ref, w0, w1, w2, w3, own_ref, send_ref, m_ref, a_ref):
        m_ref[0:share, :] = keep_ref[...]
        m_ref[share:, :] = received_ref[...]
        a_ref[...] = jnp.zeros_like(a_ref)
        for w_ref, (offset, begin, count) in zip((w0, w1, w2, w3), BUFFERS):
            for inner in range(count):
                row, column = weight_block(place_ref, offset, begin + inner)
                m = m_ref[:, pl.ds(pl.multiple_of(row * features, features), features)]
                at = pl.ds(pl.multiple_of(column * columns, columns), columns)
                a_ref[:, at] += lax.dot_general(
                    m, w_ref[inner], NT, preferred_element_type=F32
                )
        own_ref[...] = a_ref[0:share, :]
        send_ref[...] = a_ref[share:, :].astype(BF16)

    return pl.pallas_call(
        kernel,
        out_shape=(
            jax.ShapeDtypeStruct((share, 8 * columns), F32),
            jax.ShapeDtypeStruct((share, 8 * columns), BF16),
        ),
        in_specs=[pl.BlockSpec(memory_space=pltpu.SMEM)]
        + [pl.BlockSpec(memory_space=pltpu.VMEM)] * 6,
        out_specs=(pl.BlockSpec(memory_space=pltpu.VMEM),) * 2,
        scratch_shapes=[
            pltpu.VMEM((2 * share, rows), BF16),
            pltpu.VMEM((2 * share, 8 * columns), F32),
        ],
        compiler_params=pltpu.CompilerParams(vmem_limit_bytes=16 << 20),
        name="project",
    )(place, keep, received, *weights)


def widen(frozen, upstream, gain):
    def kernel(frozen_ref, upstream_ref, gain_ref, f_ref, u_ref):
        f_ref[...] = frozen_ref[...].astype(F32)
        u_ref[...] = upstream_ref[...].astype(F32) * gain_ref[...]

    shape = jax.ShapeDtypeStruct(frozen.shape, F32)
    return pl.pallas_call(
        kernel,
        out_shape=(shape, shape),
        in_specs=[pl.BlockSpec(memory_space=pltpu.VMEM)] * 3,
        out_specs=(pl.BlockSpec(memory_space=pltpu.VMEM),) * 2,
        compiler_params=pltpu.CompilerParams(vmem_limit_bytes=6 << 20),
        name="widen",
    )(frozen, upstream, gain)


def normalize(own, received, frozen, upstream, gain, block):
    share, width = own.shape

    def kernel(own_ref, received_ref, frozen_ref, up_ref, gain_ref, normed_ref, grad_ref, n_ref):
        hidden = own_ref[...] + received_ref[...].astype(F32) + frozen_ref[...]
        up = up_ref[...]
        inverse = lax.rsqrt(jnp.mean(hidden * hidden, axis=-1, keepdims=True) + EPS)
        inner = jnp.mean(up * hidden, axis=-1, keepdims=True)
        grad_ref[...] = (
            inverse * up - hidden * (inverse * inverse * inverse) * inner
        ).astype(BF16)
        normed = hidden * inverse * gain_ref[...]
        for z in range(16):
            for group in range(8):
                to, at = (z * 8 + group) * block, (group * 16 + z) * block
                n_ref[:, to : to + block] = normed[:, at : at + block]
        normed_ref[...] = n_ref[...].astype(BF16)

    shape = jax.ShapeDtypeStruct((share, width), BF16)
    return pl.pallas_call(
        kernel,
        out_shape=(shape, shape),
        in_specs=[pl.BlockSpec(memory_space=pltpu.VMEM)] * 5,
        out_specs=(pl.BlockSpec(memory_space=pltpu.VMEM),) * 2,
        scratch_shapes=[pltpu.VMEM((share, width), F32)],
        compiler_params=pltpu.CompilerParams(vmem_limit_bytes=8 << 20),
        name="normalize",
    )(own, received, frozen, upstream, gain)


def project_back(place, grad, received, weights):
    share, width = grad.shape
    _, columns, features = weights[0].shape

    def kernel(place_ref, grad_ref, received_ref, w0, w1, w2, w3, o_ref, g_ref, a_ref):
        core = place_ref[0]
        g_ref[pl.ds(pl.multiple_of(core * share, share), share), :] = grad_ref[...]
        g_ref[pl.ds(pl.multiple_of((1 - core) * share, share), share), :] = received_ref[...]
        a_ref[...] = jnp.zeros_like(a_ref)
        for w_ref, (offset, begin, count) in zip((w0, w1, w2, w3), BUFFERS):
            for inner in range(count):
                row, column = weight_block(place_ref, offset, begin + inner)
                g = g_ref[:, pl.ds(pl.multiple_of(column * columns, columns), columns)]
                a_ref[row] += jnp.dot(g, w_ref[inner], preferred_element_type=F32)
        for row in range(2):
            o_ref[:, row * features : (row + 1) * features] = a_ref[row].astype(BF16)

    return pl.pallas_call(
        kernel,
        out_shape=jax.ShapeDtypeStruct((2 * share, 2 * features), BF16),
        in_specs=[pl.BlockSpec(memory_space=pltpu.SMEM)]
        + [pl.BlockSpec(memory_space=pltpu.VMEM)] * 6,
        out_specs=pl.BlockSpec(memory_space=pltpu.VMEM),
        scratch_shapes=[
            pltpu.VMEM((2 * share, width), BF16),
            pltpu.VMEM((2, 2 * share, features), F32),
        ],
        compiler_params=pltpu.CompilerParams(vmem_limit_bytes=16 << 20),
        name="project_back",
    )(place, grad, received, *weights)


def scatter_scaled(parts, scale):
    _, tokens, rows = parts.shape
    features = rows // 2

    def kernel(scale_ref, p_ref, o_ref):
        for k in range(2):
            for row in range(2):
                at = (2 * row + k) * features
                part = p_ref[k, :, row * features : (row + 1) * features]
                o_ref[:, at : at + features] = (scale_ref[0] * part.astype(F32)).astype(BF16)

    return pl.pallas_call(
        kernel,
        out_shape=jax.ShapeDtypeStruct((2 * tokens, 2 * rows), BF16),
        grid=(2,),
        in_specs=[
            pl.BlockSpec(memory_space=pltpu.SMEM),
            pl.BlockSpec((2, tokens, rows), lambda l: (l, 0, 0)),
        ],
        out_specs=pl.BlockSpec((tokens, 2 * rows), lambda l: (l, 0)),
        compiler_params=pltpu.CompilerParams(vmem_limit_bytes=6 << 20),
        name="scatter_scaled",
    )(scale, parts)


def on_device(
    q_ctl, k_ctl, v_ctl, positions, branch_ids, cond_scale, out_weight, frozen, norm_gain, cotangent
):
    branch, core = lax.axis_index(BRANCH), lax.axis_index("k")
    y, x = lax.axis_index("y"), lax.axis_index(("h", "l"))
    share, _ = frozen.shape
    features, own = out_weight.shape
    place = jnp.stack([core, x, y]).astype(jnp.int32)
    scale = jnp.sum(
        jnp.where(jnp.arange(cond_scale.shape[0]) == branch_ids[0], cond_scale, 0.0)
    ).reshape(1)

    def to_partner(v):
        return exchange(v, lambda i: i ^ 1)

    w = jnp.broadcast_to(out_weight.T[None], (16, own, features))
    w = lax.all_to_all(w, ("c", "z"), 0, 0, tiled=True).reshape(16 * own, features)
    cosines, sines = rope_tables(positions)
    blocks = prepare(q_ctl[0], k_ctl[0], v_ctl[0], cosines, sines)
    w, blocks = lax.optimization_barrier((w, blocks))
    blocks = lax.all_to_all(blocks, CLIP, 0, 0, tiled=True)
    arrived = [exchange(w, lambda i: i ^ (r << (3 if i % 2 == 0 else 1))) for r in range(1, 4)]
    w = jnp.stack([w] + arrived)

    def along(step):
        def partner(i):
            low = 3 if i % 2 else 1
            return i + ((((i >> low) + step) & 3) - ((i >> low) & 3) << low)

        return partner

    weights = [w] + [exchange(w, along(step)) for step in (-1, 1, 2)]

    def columns_first(v):
        v = v.reshape(v.shape[0], 16, 8, own)
        return jnp.transpose(v, (0, 2, 1, 3)).reshape(v.shape[0], -1)

    gain = columns_first(norm_gain[None])
    upstream = columns_first(lax.dynamic_slice_in_dim(cotangent, branch * share, share, 0))
    frozen, upstream = widen(columns_first(frozen), upstream, gain)

    blocks, frozen, upstream, gain = lax.optimization_barrier((blocks, frozen, upstream, gain))
    core = core.astype(jnp.int32).reshape(1)
    received = to_partner(attend(blocks, scale, 1 - core))
    attended = attend(blocks, scale, core, received)
    pieces = lax.all_to_all(
        attended.reshape(HEADS * 2, share, HEAD_DIM), CLIP + ("l",), 0, 0, tiled=True
    )
    keep, send = sum_pieces(pieces, core)
    own_part, send = project(place, keep, to_partner(send), weights)
    normed, grad = normalize(own_part, to_partner(send), frozen, upstream, gain, own)
    cot = project_back(place, grad, to_partner(grad), weights)
    parts = lax.all_gather(cot, BRANCH, axis=0, tiled=False)
    grad_attn = scatter_scaled(parts, scale)
    return normed, grad_attn[None]


def solution(mesh):
    fine = Mesh(mesh.devices.reshape(8, 2, 4, 2, 2, 2), SEQ + BRANCH)

    return jax.shard_map(
        on_device,
        mesh=fine,
        in_specs=(
            P(BRANCH, SEQ, None),
            P(BRANCH, SEQ, None),
            P(BRANCH, SEQ, None),
            P(SEQ),
            P(BRANCH),
            P(),
            P(BRANCH, SEQ),
            P(SEQ + BRANCH, None),
            P(),
            P(SEQ, None),
        ),
        out_specs=(P(SEQ + BRANCH, None), P(BRANCH, SEQ, None)),
        check_vma=False,
    )
```

```python
import math

import jax
import jax.numpy as jnp
from jax import lax
from jax.experimental import pallas as pl
from jax.experimental.pallas import tpu as pltpu
from jax.sharding import Mesh
from jax.sharding import PartitionSpec as P


HEADS = 16
HEAD_DIM = 128
EPS = 1e-06
CLIP = ("z", "y", "h")
SEQ = ("c", "z", "y", "h")
BRANCH = ("l", "k")
F32 = jnp.float32
BF16 = jnp.bfloat16
NT = (((1,), (1,)), ((), ()))


def rope_tables(positions):
    exponents = jnp.arange(HEAD_DIM // 2, dtype=F32) * (2.0 / HEAD_DIM)
    angles = positions.astype(F32)[:, None] * (10000.0 ** (-exponents))
    cosines, sines = jnp.cos(angles), jnp.sin(angles)
    return (
        jnp.concatenate([cosines, cosines], axis=1),
        jnp.concatenate([-sines, sines], axis=1),
    )


def prepare(q, k, v, cosines, sines):
    rows = q.shape[0]
    factor = math.log2(math.e) / math.sqrt(HEAD_DIM)
    group = 4

    def kernel(q_ref, k_ref, v_ref, c_ref, s_ref, o_ref):
        c, s = c_ref[...], s_ref[...]
        cq, sq = c * factor, s * factor
        for g in range(group):
            at = slice(g * HEAD_DIM, (g + 1) * HEAD_DIM)
            x = q_ref[:, at].astype(F32)
            o_ref[g, 0:rows, :] = (x * cq + pltpu.roll(x, HEAD_DIM // 2, 1) * sq).astype(BF16)
            x = k_ref[:, at].astype(F32)
            o_ref[g, rows : 2 * rows, :] = (x * c + pltpu.roll(x, HEAD_DIM // 2, 1) * s).astype(BF16)
            o_ref[g, 2 * rows :, :] = v_ref[:, at]

    column = pl.BlockSpec((rows, group * HEAD_DIM), lambda i: (0, i))
    whole = pl.BlockSpec((rows, HEAD_DIM), lambda i: (0, 0))
    return pl.pallas_call(
        kernel,
        out_shape=jax.ShapeDtypeStruct((HEADS, 3 * rows, HEAD_DIM), BF16),
        grid=(HEADS // group,),
        in_specs=[column, column, column, whole, whole],
        out_specs=pl.BlockSpec((group, 3 * rows, HEAD_DIM), lambda i: (i, 0, 0)),
        compiler_params=pltpu.CompilerParams(vmem_limit_bytes=10 << 20),
        name="prepare",
    )(q, k, v, cosines, sines)


def attend(blocks, scale, part, received=None):
    sources, three_rows, _ = blocks.shape
    rows = three_rows // 3
    length = sources * rows
    share = rows // 4
    queries = length // 2
    bq, kc, kt = 384, 512, 256
    steps = queries // bq

    def kernel(part_ref, scale_ref, b_ref, *refs):
        refs = list(refs)
        r_ref = refs.pop(0) if received is not None else None
        o_ref, q_ref, k_ref, v_ref, s_ref, m_ref = refs
        for j in range(sources):
            at = slice(j * rows, (j + 1) * rows)
            for l in range(2):
                first = pl.multiple_of((2 * l + part_ref[0]) * share, share)
                to = (2 * j + l) * share
                q_ref[to : to + share, :] = b_ref[j, pl.ds(first, share), :]
            k_ref[at, :] = b_ref[j, rows : 2 * rows, :]
            v_ref[at, 0:HEAD_DIM] = b_ref[j, 2 * rows :, :]
        v_ref[:, HEAD_DIM:] = jnp.ones((length, HEAD_DIM), BF16)

        def scores(i, slot):
            q = q_ref[pl.ds(pl.multiple_of(i * bq, bq), bq), :]
            top = None
            for j in range(length // kt):
                s = lax.dot_general(
                    q, k_ref[j * kt : (j + 1) * kt, :], NT, preferred_element_type=F32
                )
                s_ref[slot, :, j * kt : (j + 1) * kt] = s
                for half in range(kt // 128):
                    piece = s[:, half * 128 : (half + 1) * 128]
                    top = piece if top is None else jnp.maximum(top, piece)
            m_ref[slot] = jnp.broadcast_to(jnp.max(top, axis=1, keepdims=True), (bq, 128))

        def mix(i, slot):
            top = jnp.concatenate([m_ref[slot]] * (kc // 128), axis=1)
            total = None
            for j in range(length // kc):
                p = jnp.exp2(s_ref[slot, :, j * kc : (j + 1) * kc] - top).astype(BF16)
                piece = jnp.dot(p, v_ref[j * kc : (j + 1) * kc, :], preferred_element_type=F32)
                total = piece if total is None else total + piece
            out = total[:, :HEAD_DIM] * (scale_ref[0] / total[:, HEAD_DIM:])
            at = pl.ds(pl.multiple_of(i * bq, bq), bq)
            if r_ref is not None:
                out = out + r_ref[at, :].astype(F32)
            o_ref[at, :] = out.astype(BF16)

        scores(0, 0)

        def pair(t, carry):
            i = 2 * t
            scores(i + 1, 1)
            mix(i, 0)
            scores(i + 2, 0)
            mix(i + 1, 1)
            return carry

        lax.fori_loop(0, (steps - 2) // 2, pair, 0)
        scores(steps - 1, 1)
        mix(steps - 2, 0)
        mix(steps - 1, 1)

    extra = () if received is None else (received,)
    return pl.pallas_call(
        kernel,
        out_shape=jax.ShapeDtypeStruct((queries, HEAD_DIM), BF16),
        in_specs=[pl.BlockSpec(memory_space=pltpu.SMEM)] * 2
        + [pl.BlockSpec(memory_space=pltpu.VMEM)] * (1 + len(extra)),
        out_specs=pl.BlockSpec(memory_space=pltpu.VMEM),
        scratch_shapes=[
            pltpu.VMEM((queries, HEAD_DIM), BF16),
            pltpu.VMEM((length, HEAD_DIM), BF16),
            pltpu.VMEM((length, 2 * HEAD_DIM), BF16),
            pltpu.VMEM((2, bq, length), F32),
            pltpu.VMEM((2, bq, 128), F32),
        ],
        compiler_params=pltpu.CompilerParams(vmem_limit_bytes=20 << 20),
        cost_estimate=pl.CostEstimate(
            flops=4 * queries * length * HEAD_DIM,
            bytes_accessed=2 * blocks.size,
            transcendentals=queries * length,
        ),
        name="attend_last" if extra else "attend_first",
    )(part, scale, blocks, *extra)


def exchange(x, partner):
    count = math.prod(lax.axis_size(name) for name in SEQ + BRANCH)
    return lax.ppermute(x, SEQ + BRANCH, [(i, partner(i)) for i in range(count)])


def sum_pieces(pieces, core):
    _, share, _ = pieces.shape

    def kernel(core_ref, p_ref, keep_ref, send_ref):
        for out, part in ((keep_ref, core_ref[0]), (send_ref, 1 - core_ref[0])):
            for block in range(2):
                for r in range(4):
                    head = (2 * block + part) * 4 + r
                    total = p_ref[2 * head].astype(F32) + p_ref[2 * head + 1].astype(F32)
                    at = (block * 4 + r) * HEAD_DIM
                    out[:, at : at + HEAD_DIM] = total.astype(BF16)

    shape = jax.ShapeDtypeStruct((share, HEADS // 2 * HEAD_DIM), BF16)
    return pl.pallas_call(
        kernel,
        out_shape=(shape, shape),
        in_specs=[
            pl.BlockSpec(memory_space=pltpu.SMEM),
            pl.BlockSpec(memory_space=pltpu.VMEM),
        ],
        out_specs=(pl.BlockSpec(memory_space=pltpu.VMEM),) * 2,
        compiler_params=pltpu.CompilerParams(vmem_limit_bytes=4 << 20),
        name="sum_pieces",
    )(core, pieces)


def weight_block(place_ref, offset, inner):
    core, x, y = place_ref[0], place_ref[1], place_ref[2]
    first = core == 0
    x_there = jnp.where(first, (x + offset) & 3, x ^ inner)
    y_there = jnp.where(first, y ^ inner, (y + offset) & 3)
    return x_there & 1, y_there * 2 + (x_there >> 1)


BUFFERS = ((0, 0, 4), (1, 0, 4), (3, 0, 4), (2, 0, 2), (2, 2, 2))


def project(place, keep, received, weights, buffers, before=None):
    share, rows = keep.shape
    _, columns, features = weights[0].shape
    count = len(weights)

    def kernel(place_ref, keep_ref, received_ref, *refs):
        w_refs, refs = refs[:count], refs[count:]
        m_ref = refs[-1]
        m_ref[0:share, :] = keep_ref[...]
        m_ref[share:, :] = received_ref[...]
        if before is None:
            a_ref = refs[0]
            a_ref[...] = jnp.zeros_like(a_ref)
        else:
            before_ref, own_ref, send_ref, a_ref = refs[:4]
            a_ref[...] = before_ref[...]
        for w_ref, (offset, begin, pieces) in zip(w_refs, buffers):
            for inner in range(pieces):
                row, column = weight_block(place_ref, offset, begin + inner)
                m = m_ref[:, pl.ds(pl.multiple_of(row * features, features), features)]
                at = pl.ds(pl.multiple_of(column * columns, columns), columns)
                a_ref[:, at] += lax.dot_general(
                    m, w_ref[inner], NT, preferred_element_type=F32
                )
        if before is not None:
            own_ref[...] = a_ref[0:share, :]
            send_ref[...] = a_ref[share:, :].astype(BF16)

    vmem = pl.BlockSpec(memory_space=pltpu.VMEM)
    total = (2 * share, 8 * columns)
    mixed = pltpu.VMEM((2 * share, rows), BF16)
    if before is None:
        extra, out = (), jax.ShapeDtypeStruct(total, F32)
        out_specs, scratch = vmem, [mixed]
    else:
        extra = (before,)
        out = (
            jax.ShapeDtypeStruct((share, 8 * columns), F32),
            jax.ShapeDtypeStruct((share, 8 * columns), BF16),
        )
        out_specs, scratch = (vmem, vmem), [pltpu.VMEM(total, F32), mixed]
    return pl.pallas_call(
        kernel,
        out_shape=out,
        in_specs=[pl.BlockSpec(memory_space=pltpu.SMEM)] + [vmem] * (2 + count + len(extra)),
        out_specs=out_specs,
        scratch_shapes=scratch,
        compiler_params=pltpu.CompilerParams(vmem_limit_bytes=16 << 20),
        name="project_near" if before is None else "project_far",
    )(place, keep, received, *weights, *extra)


def widen(frozen, upstream, gain):
    def kernel(frozen_ref, upstream_ref, gain_ref, f_ref, u_ref):
        f_ref[...] = frozen_ref[...].astype(F32)
        u_ref[...] = upstream_ref[...].astype(F32) * gain_ref[...]

    shape = jax.ShapeDtypeStruct(frozen.shape, F32)
    return pl.pallas_call(
        kernel,
        out_shape=(shape, shape),
        in_specs=[pl.BlockSpec(memory_space=pltpu.VMEM)] * 3,
        out_specs=(pl.BlockSpec(memory_space=pltpu.VMEM),) * 2,
        compiler_params=pltpu.CompilerParams(vmem_limit_bytes=6 << 20),
        name="widen",
    )(frozen, upstream, gain)


def normalize(own, received, frozen, upstream, gain, block):
    share, width = own.shape

    def kernel(own_ref, received_ref, frozen_ref, up_ref, gain_ref, normed_ref, grad_ref, n_ref):
        hidden = own_ref[...] + received_ref[...].astype(F32) + frozen_ref[...]
        up = up_ref[...]
        inverse = lax.rsqrt(jnp.mean(hidden * hidden, axis=-1, keepdims=True) + EPS)
        inner = jnp.mean(up * hidden, axis=-1, keepdims=True)
        grad_ref[...] = (
            inverse * up - hidden * (inverse * inverse * inverse) * inner
        ).astype(BF16)
        normed = hidden * inverse * gain_ref[...]
        for z in range(16):
            for group in range(8):
                to, at = (z * 8 + group) * block, (group * 16 + z) * block
                n_ref[:, to : to + block] = normed[:, at : at + block]
        normed_ref[...] = n_ref[...].astype(BF16)

    shape = jax.ShapeDtypeStruct((share, width), BF16)
    return pl.pallas_call(
        kernel,
        out_shape=(shape, shape),
        in_specs=[pl.BlockSpec(memory_space=pltpu.VMEM)] * 5,
        out_specs=(pl.BlockSpec(memory_space=pltpu.VMEM),) * 2,
        scratch_shapes=[pltpu.VMEM((share, width), F32)],
        compiler_params=pltpu.CompilerParams(vmem_limit_bytes=8 << 20),
        name="normalize",
    )(own, received, frozen, upstream, gain)


def project_back(place, grad, received, weights):
    share, width = grad.shape
    _, columns, features = weights[0].shape

    def kernel(place_ref, grad_ref, received_ref, w0, w1, w2, w3, w4, o_ref, g_ref, a_ref):
        core = place_ref[0]
        g_ref[pl.ds(pl.multiple_of(core * share, share), share), :] = grad_ref[...]
        g_ref[pl.ds(pl.multiple_of((1 - core) * share, share), share), :] = received_ref[...]
        a_ref[...] = jnp.zeros_like(a_ref)
        for w_ref, (offset, begin, count) in zip((w0, w1, w2, w3, w4), BUFFERS):
            for inner in range(count):
                row, column = weight_block(place_ref, offset, begin + inner)
                g = g_ref[:, pl.ds(pl.multiple_of(column * columns, columns), columns)]
                a_ref[row] += jnp.dot(g, w_ref[inner], preferred_element_type=F32)
        for row in range(2):
            o_ref[:, row * features : (row + 1) * features] = a_ref[row].astype(BF16)

    return pl.pallas_call(
        kernel,
        out_shape=jax.ShapeDtypeStruct((2 * share, 2 * features), BF16),
        in_specs=[pl.BlockSpec(memory_space=pltpu.SMEM)]
        + [pl.BlockSpec(memory_space=pltpu.VMEM)] * 7,
        out_specs=pl.BlockSpec(memory_space=pltpu.VMEM),
        scratch_shapes=[
            pltpu.VMEM((2 * share, width), BF16),
            pltpu.VMEM((2, 2 * share, features), F32),
        ],
        compiler_params=pltpu.CompilerParams(vmem_limit_bytes=16 << 20),
        name="project_back",
    )(place, grad, received, *weights)


def scatter_scaled(parts, scale):
    _, tokens, rows = parts.shape
    features = rows // 2

    def kernel(scale_ref, p_ref, o_ref):
        for k in range(2):
            for row in range(2):
                at = (2 * row + k) * features
                part = p_ref[k, :, row * features : (row + 1) * features]
                o_ref[:, at : at + features] = (scale_ref[0] * part.astype(F32)).astype(BF16)

    return pl.pallas_call(
        kernel,
        out_shape=jax.ShapeDtypeStruct((2 * tokens, 2 * rows), BF16),
        grid=(2,),
        in_specs=[
            pl.BlockSpec(memory_space=pltpu.SMEM),
            pl.BlockSpec((2, tokens, rows), lambda l: (l, 0, 0)),
        ],
        out_specs=pl.BlockSpec((tokens, 2 * rows), lambda l: (l, 0)),
        compiler_params=pltpu.CompilerParams(vmem_limit_bytes=6 << 20),
        name="scatter_scaled",
    )(scale, parts)


def on_device(
    q_ctl, k_ctl, v_ctl, positions, branch_ids, cond_scale, out_weight, frozen, norm_gain, cotangent
):
    branch, core = lax.axis_index(BRANCH), lax.axis_index("k")
    y, x = lax.axis_index("y"), lax.axis_index(("h", "l"))
    share, _ = frozen.shape
    features, own = out_weight.shape
    place = jnp.stack([core, x, y]).astype(jnp.int32)
    scale = jnp.sum(
        jnp.where(jnp.arange(cond_scale.shape[0]) == branch_ids[0], cond_scale, 0.0)
    ).reshape(1)

    def to_partner(v):
        return exchange(v, lambda i: i ^ 1)

    w = jnp.broadcast_to(out_weight.T[None], (16, own, features))
    w = lax.all_to_all(w, ("c", "z"), 0, 0, tiled=True).reshape(16 * own, features)
    cosines, sines = rope_tables(positions)
    blocks = prepare(q_ctl[0], k_ctl[0], v_ctl[0], cosines, sines)
    w, blocks = lax.optimization_barrier((w, blocks))
    blocks = lax.all_to_all(blocks, CLIP, 0, 0, tiled=True)
    arrived = [exchange(w, lambda i: i ^ (r << (3 if i % 2 == 0 else 1))) for r in range(1, 4)]
    w = jnp.stack([w] + arrived)

    def along(step):
        def partner(i):
            low = 3 if i % 2 else 1
            return i + ((((i >> low) + step) & 3) - ((i >> low) & 3) << low)

        return partner

    up, down = exchange(w, along(-1)), exchange(w, along(1))
    weights = [w, up, down, exchange(up[:2], along(-1)), exchange(down[2:], along(1))]

    def columns_first(v):
        v = v.reshape(v.shape[0], 16, 8, own)
        return jnp.transpose(v, (0, 2, 1, 3)).reshape(v.shape[0], -1)

    gain = columns_first(norm_gain[None])
    upstream = columns_first(lax.dynamic_slice_in_dim(cotangent, branch * share, share, 0))
    frozen, upstream = widen(columns_first(frozen), upstream, gain)

    blocks, frozen, upstream, gain = lax.optimization_barrier((blocks, frozen, upstream, gain))
    core = core.astype(jnp.int32).reshape(1)
    received = to_partner(attend(blocks, scale, 1 - core))
    attended = attend(blocks, scale, core, received)
    pieces = lax.all_to_all(
        attended.reshape(HEADS * 2, share, HEAD_DIM), CLIP + ("l",), 0, 0, tiled=True
    )
    keep, send = sum_pieces(pieces, core)
    received = to_partner(send)
    near = project(place, keep, received, weights[:3], BUFFERS[:3])
    own_part, send = project(place, keep, received, weights[3:], BUFFERS[3:], near)
    normed, grad = normalize(own_part, to_partner(send), frozen, upstream, gain, own)
    cot = project_back(place, grad, to_partner(grad), weights)
    parts = lax.all_gather(cot, BRANCH, axis=0, tiled=False)
    grad_attn = scatter_scaled(parts, scale)
    return normed, grad_attn[None]


def solution(mesh):
    fine = Mesh(mesh.devices.reshape(8, 2, 4, 2, 2, 2), SEQ + BRANCH)

    return jax.shard_map(
        on_device,
        mesh=fine,
        in_specs=(
            P(BRANCH, SEQ, None),
            P(BRANCH, SEQ, None),
            P(BRANCH, SEQ, None),
            P(SEQ),
            P(BRANCH),
            P(),
            P(BRANCH, SEQ),
            P(SEQ + BRANCH, None),
            P(),
            P(SEQ, None),
        ),
        out_specs=(P(SEQ + BRANCH, None), P(BRANCH, SEQ, None)),
        check_vma=False,
    )
```
